512 devices in a mesh: row: 32 (over z, y_hi), col: 16 (over y_lo, x, core).
Axes of the slice: x: 4, y: 8 (y_hi: 4, y_lo: 2; y = y_hi * 2 + y_lo), z: 8, core: 2. Of those that a mesh axis runs over, the one named last changes fastest.
Arguments:
- signal: float32 [32, 65536], P(None, 'row'), may hold values from -8 to 8
- tile_values: bfloat16 [32, 16, 64, 128, 128], P('row', 'col'), may hold values from 1e-12 to 1, as said below
- tile_places: int32 [32, 16, 2, 64], P('row', 'col'), may hold values from 0 to 31, as said below
- tile_counts: int32 [32, 16], P('row', 'col'), may hold values from 16 to 64, as said below
Outputs:
- first_wavelet: float32 [32, 65536], P(None, 'row')
- second_wavelet: float32 [32, 65536], P(None, 'row')
- lowpass: float32 [32, 65536], P(None, 'row')
The draws below stay inside these ranges and needn't reach their ends.
Inputs may be any that keep to these rules, and one draw needn't show every extreme that they name: `tile_values`: A is symmetric, and every node's row of A has a positive entry on the diagonal. Slots at or after a device's count hold tiles that are not part of A. `tile_places`: place 0 lies below 16, place 1 below 32; the live slots of one device name distinct places. `tile_counts`: some device is full in every draw.
All inputs are finite; a program needn't handle non-finite values.
Results may differ from the reference program's by a relative error of at most 0.0003.
Values may be sent and summed in bfloat16 or wider, within the bound.
No kernel may reach another device: no remote copies, remote signals or barrier semaphores. Data moves between devices by JAX's collectives and lax.ppermute only.
A program may use at most 64 MiB of HBM per device.

```python
import math
import jax
import jax.numpy as jnp
from jax import lax

CH = 32
TILE = 128
NODES = 65536
TILE_ROWS = 16
SQUARE_TILES = 32
K_SLOTS = 64
N_ROW = 32
N_COL = 16


def square_list(base, first, second):
    cells = TILE_ROWS * TILE_ROWS
    grid = jnp.arange(cells, dtype=jnp.int32)
    cell_row = grid // TILE_ROWS
    cell_col = grid % TILE_ROWS
    along = jnp.arange(TILE_ROWS, dtype=jnp.int32)
    low = jnp.minimum(first, second)
    high = jnp.maximum(first, second)
    pair_id = low * N_ROW + high
    order = jax.random.permutation(jax.random.fold_in(base, pair_id), cells).astype(jnp.int32)
    perm_row = cell_row[order]
    perm_col = cell_col[order]
    score = jnp.where(perm_row < perm_col, 0, cells) + grid
    pick = jnp.argsort(score)[:TILE_ROWS // 2]
    upper_row = perm_row[pick]
    upper_col = perm_col[pick]
    diag_row = jnp.concatenate([along, upper_row, upper_col])
    diag_col = jnp.concatenate([along, upper_col, upper_row])
    drawn_row = perm_row[:SQUARE_TILES]
    drawn_col = perm_col[:SQUARE_TILES]
    flip = first > second
    off_row = jnp.where(flip, drawn_col, drawn_row)
    off_col = jnp.where(flip, drawn_row, drawn_col)
    same = first == second
    list_row = jnp.where(same, diag_row, off_row)
    list_col = jnp.where(same, diag_col, off_col)
    gap = jnp.minimum((first - second) % N_ROW, (second - first) % N_ROW)
    extra = jax.random.randint(jax.random.fold_in(base, pair_id + 7 * N_ROW * N_ROW), (), 0, TILE_ROWS // 2 + 1).astype(jnp.int32)
    live_number = jnp.where(gap <= 1, SQUARE_TILES, TILE_ROWS // 2 + extra)
    return (list_row, list_col, live_number)


def device_layout(base, row_block, col_block):
    rows_a, cols_a, count_a = square_list(base, row_block, 2 * col_block)
    rows_b, cols_b, count_b = square_list(base, row_block, 2 * col_block + 1)
    position = jnp.arange(SQUARE_TILES, dtype=jnp.int32)
    live_slot = jnp.concatenate([position < count_a, position < count_b])
    slot_row = jnp.concatenate([rows_a, rows_b])
    slot_col = jnp.concatenate([cols_a, cols_b + TILE_ROWS])
    squares = jnp.concatenate([jnp.full((SQUARE_TILES,), 2 * col_block, jnp.int32), jnp.full((SQUARE_TILES,), 2 * col_block + 1, jnp.int32)])
    order = jnp.argsort(jnp.where(live_slot, 0, K_SLOTS) + jnp.arange(K_SLOTS, dtype=jnp.int32))
    return (slot_row[order], slot_col[order], squares[order], count_a + count_b)


def graph_layouts(key):
    base = jax.random.fold_in(key, 11)
    device_ids = jnp.arange(N_ROW * N_COL, dtype=jnp.int32)

    def one_device(index):
        slot_row, slot_col, squares, count = device_layout(base, index // N_COL, index % N_COL)
        return (jnp.stack([slot_row, slot_col]), count)
    places, counts = lax.map(one_device, device_ids)
    return (places.reshape(N_ROW, N_COL, 2, K_SLOTS), counts.reshape(N_ROW, N_COL))


def draw_tile_places(key, part):
    return graph_layouts(jax.random.fold_in(key, 5))[0]


def draw_tile_counts(key, part):
    return graph_layouts(jax.random.fold_in(key, 5))[1]


def draw_tile_values(key, part):
    graph_key = jax.random.fold_in(key, 5)
    base = jax.random.fold_in(graph_key, 11)
    value_key = jax.random.fold_in(graph_key, 29)
    total_tiles = N_ROW * TILE_ROWS
    inner = jnp.arange(TILE, dtype=jnp.int32)
    lower_half = inner[:, None] <= inner[None, :]

    def one_tile(global_row, global_col):
        pair = jnp.minimum(global_row, global_col) * total_tiles + jnp.maximum(global_row, global_col)
        raw = jnp.exp(jax.random.uniform(jax.random.fold_in(value_key, pair), (TILE, TILE), jnp.float32, math.log(1e-12), 0.0))
        symmetric = jnp.where(lower_half, raw, raw.T)
        picked = jnp.where(global_row < global_col, raw, jnp.where(global_row > global_col, raw.T, symmetric))
        return picked.astype(jnp.bfloat16)

    def one_device(index):
        row_block = index // N_COL
        col_block = index % N_COL
        slot_row, slot_col, squares, count = device_layout(base, row_block, col_block)
        global_row = row_block * TILE_ROWS + slot_row
        global_col = squares * TILE_ROWS + slot_col % TILE_ROWS
        return jax.vmap(one_tile)(global_row, global_col)
    values = lax.map(one_device, jnp.arange(N_ROW * N_COL, dtype=jnp.int32))
    return values.reshape(N_ROW, N_COL, K_SLOTS, TILE, TILE)


def draw_signal(key, part):
    key_rough = jax.random.fold_in(key, 0)
    rough = jax.random.normal(key_rough, (CH, NODES), jnp.float32) * 1.5
    return jnp.clip(rough, -8.0, 8.0)


def setup_inputs(seed: int = 0) -> dict:
    splits = jax.random.split(jax.random.key(seed), 5)
    signal = draw_signal(jax.random.fold_in(splits[4], 71), 0)
    tile_values = draw_tile_values(jax.random.fold_in(splits[4], 71), 0)
    tile_places = draw_tile_places(jax.random.fold_in(splits[4], 71), 0)
    tile_counts = draw_tile_counts(jax.random.fold_in(splits[4], 71), 0)
    return {"signal": signal, "tile_values": tile_values, "tile_places": tile_places, "tile_counts": tile_counts}


highest_precision = lax.Precision.HIGHEST


def reference(signal, tile_values, tile_places, tile_counts):
    halves = N_ROW // N_COL
    row_len = TILE_ROWS * TILE
    col_len = halves * row_len
    slot_ids = jnp.arange(K_SLOTS, dtype=jnp.int32)
    row_ids = jnp.arange(TILE_ROWS, dtype=jnp.int32)

    def live_rows(row_block, col_block):
        live_slot = (slot_ids < tile_counts[row_block, col_block]).astype(jnp.float32)
        places = tile_places[row_block, col_block]
        return (places[0][:, None] == row_ids[None, :]).astype(jnp.float32) * live_slot[:, None]

    def block_degree(row_block):
        def per_col(running, col_block):
            sums = jnp.sum(tile_values[row_block, col_block].astype(jnp.float32), axis=2)
            row_hot = live_rows(row_block, col_block)
            return running + jnp.einsum("kt,ka->ta", row_hot, sums, precision=highest_precision), None
        running, _ = lax.scan(per_col, jnp.zeros((TILE_ROWS, TILE), jnp.float32), jnp.arange(N_COL, dtype=jnp.int32))
        return running.reshape(row_len)

    degree = lax.map(block_degree, jnp.arange(N_ROW, dtype=jnp.int32)).reshape(NODES)

    def walk(vector):
        rounded = (vector / degree[None, :]).astype(jnp.bfloat16)
        scaled = lax.optimization_barrier(rounded).astype(jnp.float32)

        def block_apply(row_block):
            def per_col(running, col_block):
                column = lax.dynamic_slice_in_dim(scaled, col_block * col_len, col_len, 1)
                column = column.reshape(CH, halves * TILE_ROWS, TILE)
                picked = jnp.take(column, tile_places[row_block, col_block, 1], axis=1)
                blocks = tile_values[row_block, col_block].astype(jnp.float32)
                products = jnp.einsum("kab,ckb->cka", blocks, picked, precision=highest_precision)
                row_hot = live_rows(row_block, col_block)
                return running + jnp.einsum("cka,kt->cta", products, row_hot, precision=highest_precision), None
            running, _ = lax.scan(per_col, jnp.zeros((CH, TILE_ROWS, TILE), jnp.float32), jnp.arange(N_COL, dtype=jnp.int32))
            return running.reshape(CH, row_len)

        row_parts = lax.map(block_apply, jnp.arange(N_ROW, dtype=jnp.int32))
        spread = jnp.transpose(row_parts, (1, 0, 2)).reshape(CH, NODES)
        return 0.5 * (vector + spread)

    walked = walk(signal)
    lowpass = walk(walked)
    return jnp.abs(signal - walked), jnp.abs(walked - lowpass), lowpass
```

```python
import jax
import jax.numpy as jnp
from jax import lax
from jax.sharding import PartitionSpec as P

highest_precision = lax.Precision.HIGHEST


def to_columns(scaled, row_size, col_size):
    halves = row_size // col_size
    received = []
    for turn in range(halves):
        pairs = []
        for row in range(row_size):
            for col in range(col_size):
                target_row = halves * col + (turn + row) % halves
                pairs.append((row * col_size + col, target_row * col_size + row // halves))
        received.append(lax.ppermute(scaled, ("row", "col"), pairs))
    return jnp.concatenate(received, axis=0)


def reduce_scatter(partials):
    return jnp.sum(lax.all_to_all(partials, "col", 0, 0, tiled=True), axis=0)


def all_gather(piece, size):
    return lax.all_to_all(jnp.broadcast_to(piece[None], (size,) + piece.shape), "col", 0, 0, tiled=True)


def on_device(signal, tile_values, tile_places, tile_counts):
    channels, row_len = signal.shape
    slot_count = tile_values.shape[2]
    tile_width = tile_values.shape[3]
    tile_rows = row_len // tile_width
    row_size = lax.axis_size("row")
    col_size = lax.axis_size("col")
    halves = row_size // col_size
    row_index = lax.axis_index("row")
    col_index = lax.axis_index("col")
    blocks = tile_values.reshape(slot_count, tile_width, tile_width)
    places = tile_places.reshape(2, slot_count)
    live_count = tile_counts.reshape(())
    live_slot = (lax.iota(jnp.int32, slot_count) < live_count).astype(jnp.float32)
    row_hot = (places[0][:, None] == lax.iota(jnp.int32, tile_rows)[None, :]).astype(
        jnp.float32
    ) * live_slot[:, None]
    half_of = (places[1] // tile_rows + halves - row_index % halves) % halves
    pick = half_of * tile_rows + places[1] % tile_rows

    signal = signal.reshape(channels, tile_rows, tile_width).transpose(1, 0, 2)
    signal_piece = lax.dynamic_index_in_dim(signal, col_index, 0, keepdims=False)

    sums = jnp.sum(blocks, axis=2, dtype=jnp.float32)
    degree_part = jnp.einsum("kt,ka->ta", row_hot, sums, precision=highest_precision)
    degree = jnp.sum(all_gather(degree_part, col_size).reshape(col_size, tile_rows, tile_width), axis=0)

    def walk(vector, piece):
        scaled = (vector / degree[:, None, :]).astype(jnp.bfloat16)
        column = to_columns(scaled, row_size, col_size)
        picked = jnp.take(column, pick, axis=0)
        products = jnp.einsum("kab,kcb->kca", blocks, picked, preferred_element_type=jnp.float32)
        partials = jnp.einsum("kca,kt->tca", products, row_hot, precision=highest_precision)
        spread = reduce_scatter(partials)
        return 0.5 * (piece + spread)

    walked_piece = walk(signal, signal_piece)
    walked = all_gather(walked_piece, col_size).reshape(tile_rows, channels, tile_width)
    lowpass_piece = walk(walked, walked_piece)
    lowpass = all_gather(lowpass_piece, col_size).reshape(tile_rows, channels, tile_width)

    def back(array):
        return array.transpose(1, 0, 2).reshape(channels, row_len)

    return (back(jnp.abs(signal - walked)), back(jnp.abs(walked - lowpass)), back(lowpass))


def solution(mesh):
    in_specs = (
        P(None, "row"),
        P("row", "col", None, None, None),
        P("row", "col", None, None),
        P("row", "col"),
    )
    out_specs = (P(None, "row"), P(None, "row"), P(None, "row"))
    return jax.shard_map(
        on_device, mesh=mesh, in_specs=in_specs, out_specs=out_specs, check_vma=False
    )
```

```python
import jax
import jax.numpy as jnp
from jax import lax
from jax.sharding import PartitionSpec as P

highest_precision = lax.Precision.HIGHEST


def exchange(partials, axis):
    return lax.all_to_all(partials, axis, 0, 0, tiled=True)


def all_gather(piece, axis):
    return exchange(jnp.broadcast_to(piece[None], (lax.axis_size(axis),) + piece.shape), axis)


def on_device(signal, tile_values, tile_places, tile_counts):
    channels, row_len = signal.shape
    slot_count = tile_values.shape[2]
    tile_width = tile_values.shape[3]
    tile_rows = row_len // tile_width
    row_size = lax.axis_size("row")
    col_size = lax.axis_size("col")
    halves = row_size // col_size
    col_index = lax.axis_index("col")
    blocks = tile_values.reshape(slot_count, tile_width, tile_width)
    places = tile_places.reshape(2, slot_count)
    live_count = tile_counts.reshape(())
    live_slot = (lax.iota(jnp.int32, slot_count) < live_count).astype(jnp.float32)
    row_hot = (places[0][:, None] == lax.iota(jnp.int32, tile_rows)[None, :]).astype(
        jnp.float32
    ) * live_slot[:, None]
    col_hot = (places[1][:, None] == lax.iota(jnp.int32, halves * tile_rows)[None, :]).astype(
        jnp.float32
    ) * live_slot[:, None]
    to_column = [
        (row * col_size + col, ((row % halves) * tile_rows + col) * col_size + row // halves)
        for row in range(row_size)
        for col in range(col_size)
    ]
    to_row = [(target, source) for source, target in to_column]

    signal = signal.reshape(channels, tile_rows, tile_width).transpose(1, 0, 2)
    signal_piece = lax.ppermute(
        lax.dynamic_index_in_dim(signal, col_index, 0, keepdims=False), ("row", "col"), to_column
    )

    sums = jnp.sum(blocks, axis=2, dtype=jnp.float32)
    degree_part = jnp.einsum("kt,ka->ta", row_hot, sums, precision=highest_precision)
    degree = jnp.sum(all_gather(degree_part, "col").reshape(col_size, tile_rows, tile_width), axis=0)
    degree_piece = lax.ppermute(
        lax.dynamic_index_in_dim(degree, col_index, 0, keepdims=True), ("row", "col"), to_column
    )

    scaled = (signal / degree[:, None, :]).astype(jnp.bfloat16)
    picked = jnp.take(scaled, places[0], axis=0)
    products = jnp.einsum("kab,kca->kcb", blocks, picked, preferred_element_type=jnp.float32)
    partials = jnp.einsum("kcb,kt->tcb", products, col_hot, precision=highest_precision)
    spread = jnp.sum(exchange(partials, "row"), axis=0)
    walked_piece = 0.5 * (signal_piece + spread)

    scaled = (walked_piece / degree_piece).astype(jnp.bfloat16)
    column = all_gather(scaled, "row").reshape(halves * tile_rows, channels, tile_width)
    walked_piece = lax.ppermute(walked_piece, ("row", "col"), to_row)
    picked = jnp.take(column, places[1], axis=0)
    products = jnp.einsum("kab,kcb->kca", blocks, picked, preferred_element_type=jnp.float32)
    partials = jnp.einsum("kca,kt->tca", products, row_hot, precision=highest_precision)
    spread = jnp.sum(exchange(partials, "col"), axis=0)
    lowpass_piece = 0.5 * (walked_piece + spread)

    both = all_gather(jnp.stack([walked_piece, lowpass_piece]), "col")
    both = both.reshape(tile_rows, 2, channels, tile_width)
    walked = both[:, 0]
    lowpass = both[:, 1]

    def back(array):
        return array.transpose(1, 0, 2).reshape(channels, row_len)

    return (back(jnp.abs(signal - walked)), back(jnp.abs(walked - lowpass)), back(lowpass))


def solution(mesh):
    in_specs = (
        P(None, "row"),
        P("row", "col", None, None, None),
        P("row", "col", None, None),
        P("row", "col"),
    )
    out_specs = (P(None, "row"), P(None, "row"), P(None, "row"))
    return jax.shard_map(
        on_device, mesh=mesh, in_specs=in_specs, out_specs=out_specs, check_vma=False
    )
```

```python
import functools

import jax
import jax.numpy as jnp
from jax import lax
from jax.experimental import pallas as pl
from jax.experimental.pallas import tpu as pltpu
from jax.sharding import PartitionSpec as P

CHUNKS = 8
VMEM_BYTES = 12 * 1024 * 1024


def exchange(partials, axis):
    return lax.all_to_all(partials, axis, 0, 0, tiled=True)


def all_gather(piece, axis):
    return exchange(jnp.broadcast_to(piece[None], (lax.axis_size(axis),) + piece.shape), axis)


def place(places, which, slot):
    return places[0, 0, which, slot]


def degree_kernel(places, counts, tiles, held, out, sems):
    slot_count = tiles.shape[2]
    step = slot_count // CHUNKS
    copies = []
    for chunk in range(CHUNKS):
        span = pl.ds(chunk * step, step)
        copies.append(pltpu.make_async_copy(tiles.at[0, 0, span], held.at[span], sems.at[chunk]))
        copies[-1].start()
    rows, width = out.shape[1:]
    ids = lax.broadcasted_iota(jnp.int32, (rows, width), 0)
    total = jnp.zeros((rows, width), jnp.float32)
    for slot in range(slot_count):
        if slot % step == 0:
            copies[slot // step].wait()
        row = jnp.where(slot < counts[0, 0], place(places, 0, slot), rows)
        hot = jnp.where(ids == row, 1.0, 0.0).astype(jnp.bfloat16)
        total += lax.dot_general(
            hot, held[slot], (((1,), (1,)), ((), ())), preferred_element_type=jnp.float32
        )
    for target in range(out.shape[0]):
        out[target] = total


def first_kernel(halves, places, counts, signal, gathered, held, out, piece, scaled, degree):
    slot_count, width, _ = held.shape
    rows = gathered.shape[1]
    row_index = lax.axis_index("row")
    col_index = lax.axis_index("col")
    total = gathered[0]
    for source in range(1, gathered.shape[0]):
        total += gathered[source]
    degree[...] = total
    piece[...] = degree[pl.ds(col_index, 1), :]
    for tile in range(rows):
        block = signal[:, tile * width : (tile + 1) * width]
        scaled[tile] = (block / degree[tile : tile + 1, :]).astype(jnp.bfloat16)
        for half in range(halves):
            own = row_index == col_index * halves + half
            out[half * rows + tile] = jnp.where(own, block, 0.0)
    for slot in range(slot_count):
        left = scaled[place(places, 0, slot)]
        left = jnp.where(slot < counts[0, 0], left, jnp.zeros_like(left))
        target = place(places, 1, slot)
        out[target] += lax.dot_general(
            left, held[slot], (((1,), (0,)), ((), ())), preferred_element_type=jnp.float32
        )


def second_kernel(places, counts, column, held, out):
    for tile in range(out.shape[0]):
        out[tile] = jnp.zeros(out.shape[1:], jnp.float32)
    for slot in range(held.shape[0]):
        left = column[place(places, 1, slot)]
        left = jnp.where(slot < counts[0, 0], left, jnp.zeros_like(left))
        target = place(places, 0, slot)
        out[target] += lax.dot_general(
            left, held[slot], (((1,), (1,)), ((), ())), preferred_element_type=jnp.float32
        )


def output_kernel(signal, both, first, second, low):
    rows, _, _, width = both.shape
    for tile in range(rows):
        span = slice(tile * width, (tile + 1) * width)
        walked = both[tile, 0]
        lowpass = both[tile, 1]
        first[:, span] = jnp.abs(signal[:, span] - walked)
        second[:, span] = jnp.abs(walked - lowpass)
        low[:, span] = lowpass


def in_vmem():
    return pl.BlockSpec(memory_space=pltpu.VMEM)


def in_smem():
    return pl.BlockSpec(memory_space=pltpu.SMEM)


def on_device(signal, tile_values, tile_places, tile_counts):
    channels, row_len = signal.shape
    slot_count, width = tile_values.shape[2:4]
    rows = row_len // width
    row_size = lax.axis_size("row")
    col_size = lax.axis_size("col")
    halves = row_size // col_size
    params = pltpu.CompilerParams(vmem_limit_bytes=VMEM_BYTES)
    to_column = [
        (row * col_size + col, ((row % halves) * rows + col) * col_size + row // halves)
        for row in range(row_size)
        for col in range(col_size)
    ]
    to_row = [(target, source) for source, target in to_column]

    held, degree_part = pl.pallas_call(
        degree_kernel,
        out_shape=(
            pltpu.VMEM((slot_count, width, width), jnp.bfloat16),
            jax.ShapeDtypeStruct((col_size, rows, width), jnp.float32),
        ),
        in_specs=[in_smem(), in_smem(), pl.BlockSpec(memory_space=pltpu.HBM)],
        out_specs=(in_vmem(), in_vmem()),
        scratch_shapes=[pltpu.SemaphoreType.DMA((CHUNKS,))],
        compiler_params=params,
        name="degree",
    )(tile_places, tile_counts, tile_values)
    gathered = exchange(degree_part, "col")

    partials, degree_piece = pl.pallas_call(
        functools.partial(first_kernel, halves),
        out_shape=(
            jax.ShapeDtypeStruct((halves * rows, channels, width), jnp.float32),
            jax.ShapeDtypeStruct((1, width), jnp.float32),
        ),
        in_specs=[in_smem(), in_smem(), in_vmem(), in_vmem(), in_vmem()],
        out_specs=(in_vmem(), in_vmem()),
        scratch_shapes=[
            pltpu.VMEM((rows, channels, width), jnp.bfloat16),
            pltpu.VMEM((rows, width), jnp.float32),
        ],
        compiler_params=params,
        name="first",
    )(tile_places, tile_counts, signal, gathered, held)
    received = exchange(partials, "row")
    degree_piece = lax.ppermute(degree_piece, ("row", "col"), to_column)
    walked_piece = 0.5 * jnp.sum(received, axis=0)
    scaled = (walked_piece / degree_piece).astype(jnp.bfloat16)

    column = all_gather(scaled, "row").reshape(halves * rows, channels, width)
    walked_piece = lax.ppermute(walked_piece, ("row", "col"), to_row)
    column, walked_piece = lax.optimization_barrier((column, walked_piece))
    partials = pl.pallas_call(
        second_kernel,
        out_shape=jax.ShapeDtypeStruct((rows, channels, width), jnp.float32),
        in_specs=[in_smem(), in_smem(), in_vmem(), in_vmem()],
        out_specs=in_vmem(),
        compiler_params=params,
        name="second",
    )(tile_places, tile_counts, column, held)
    spread = jnp.sum(exchange(partials, "col"), axis=0)
    lowpass_piece = 0.5 * (walked_piece + spread)

    both = all_gather(jnp.stack([walked_piece, lowpass_piece]), "col")
    both = both.reshape(rows, 2, channels, width)
    return pl.pallas_call(
        output_kernel,
        out_shape=(jax.ShapeDtypeStruct((channels, row_len), jnp.float32),) * 3,
        in_specs=[in_vmem(), in_vmem()],
        out_specs=(in_vmem(),) * 3,
        compiler_params=params,
        name="outputs",
    )(signal, both)


def solution(mesh):
    in_specs = (
        P(None, "row"),
        P("row", "col", None, None, None),
        P("row", "col", None, None),
        P("row", "col"),
    )
    out_specs = (P(None, "row"), P(None, "row"), P(None, "row"))
    return jax.shard_map(
        on_device, mesh=mesh, in_specs=in_specs, out_specs=out_specs, check_vma=False
    )
```

```python
import functools

import jax
import jax.numpy as jnp
from jax import lax
from jax.experimental import pallas as pl
from jax.experimental.pallas import tpu as pltpu
from jax.sharding import PartitionSpec as P

CHUNKS = 8
VMEM_BYTES = 12 * 1024 * 1024


def exchange(partials, axis):
    return lax.all_to_all(partials, axis, 0, 0, tiled=True)


def all_gather(piece, axis):
    return exchange(jnp.broadcast_to(piece[None], (lax.axis_size(axis),) + piece.shape), axis)


def place(places, which, slot):
    return places[0, 0, which, slot]


def degree_kernel(counts, places_hbm, tiles, held, out, places, sums, small, sems):
    slot_count = tiles.shape[2]
    copy_places = pltpu.make_async_copy(places_hbm, places, small)
    copy_places.start()
    step = slot_count // CHUNKS
    copies = []
    for chunk in range(CHUNKS):
        span = pl.ds(chunk * step, step)
        copies.append(pltpu.make_async_copy(tiles.at[0, 0, span], held.at[span], sems.at[chunk]))
        copies[-1].start()
    targets, rows, width = out.shape
    sums[...] = jnp.zeros_like(sums)
    ones = jnp.ones((8, width), jnp.bfloat16)
    copy_places.wait()
    for chunk in range(CHUNKS):
        copies[chunk].wait()
        block = held[chunk * step : (chunk + 1) * step].reshape(step * width, width)
        found = lax.dot_general(
            ones, block, (((1,), (1,)), ((), ())), preferred_element_type=jnp.float32
        )
        for index in range(step):
            slot = chunk * step + index
            row = jnp.where(slot < counts[0, 0], place(places, 0, slot), rows)
            sums[row] += found[:, index * width : (index + 1) * width]
    for row in range(rows):
        for target in range(targets):
            out[target, row : row + 1, :] = sums[row, 0:1, :]


def first_kernel(halves, places, counts, signal, gathered, held, out, piece, scaled, degree):
    slot_count, width, _ = held.shape
    rows = gathered.shape[1]
    row_index = lax.axis_index("row")
    col_index = lax.axis_index("col")
    total = gathered[0]
    for source in range(1, gathered.shape[0]):
        total += gathered[source]
    degree[...] = total
    piece[...] = degree[pl.ds(col_index, 1), :]
    for tile in range(rows):
        block = signal[:, tile * width : (tile + 1) * width]
        scaled[tile] = (block / degree[tile : tile + 1, :]).astype(jnp.bfloat16)
        for half in range(halves):
            own = row_index == col_index * halves + half
            out[half * rows + tile] = jnp.where(own, block, 0.0)
    for slot in range(slot_count):
        left = scaled[place(places, 0, slot)]
        left = jnp.where(slot < counts[0, 0], left, jnp.zeros_like(left))
        target = place(places, 1, slot)
        out[target] += lax.dot_general(
            left, held[slot], (((1,), (0,)), ((), ())), preferred_element_type=jnp.float32
        )


def second_kernel(places, counts, column, held, out):
    for tile in range(out.shape[0]):
        out[tile] = jnp.zeros(out.shape[1:], jnp.float32)
    for slot in range(held.shape[0]):
        left = column[place(places, 1, slot)]
        left = jnp.where(slot < counts[0, 0], left, jnp.zeros_like(left))
        target = place(places, 0, slot)
        out[target] += lax.dot_general(
            left, held[slot], (((1,), (1,)), ((), ())), preferred_element_type=jnp.float32
        )


def output_kernel(signal, both, first, second, low):
    rows, _, _, width = both.shape
    for tile in range(rows):
        span = slice(tile * width, (tile + 1) * width)
        walked = both[tile, 0]
        lowpass = both[tile, 1]
        first[:, span] = jnp.abs(signal[:, span] - walked)
        second[:, span] = jnp.abs(walked - lowpass)
        low[:, span] = lowpass


def in_vmem():
    return pl.BlockSpec(memory_space=pltpu.VMEM)


def in_smem():
    return pl.BlockSpec(memory_space=pltpu.SMEM)


def on_device(signal, tile_values, tile_places, tile_counts):
    channels, row_len = signal.shape
    slot_count, width = tile_values.shape[2:4]
    rows = row_len // width
    row_size = lax.axis_size("row")
    col_size = lax.axis_size("col")
    halves = row_size // col_size
    params = pltpu.CompilerParams(vmem_limit_bytes=VMEM_BYTES)
    to_column = [
        (row * col_size + col, ((row % halves) * rows + col) * col_size + row // halves)
        for row in range(row_size)
        for col in range(col_size)
    ]
    to_row = [(target, source) for source, target in to_column]

    held, degree_part, places = pl.pallas_call(
        degree_kernel,
        out_shape=(
            pltpu.VMEM((slot_count, width, width), jnp.bfloat16),
            jax.ShapeDtypeStruct((col_size, rows, width), jnp.float32),
            pltpu.SMEM(tile_places.shape, jnp.int32),
        ),
        in_specs=[in_smem()] + [pl.BlockSpec(memory_space=pltpu.HBM)] * 2,
        out_specs=(in_vmem(), in_vmem(), in_smem()),
        scratch_shapes=[
            pltpu.VMEM((rows + 1, 8, width), jnp.float32),
            pltpu.SemaphoreType.DMA,
            pltpu.SemaphoreType.DMA((CHUNKS,)),
        ],
        compiler_params=params,
        name="degree",
    )(
        tile_counts,
        pltpu.with_memory_space_constraint(tile_places, pltpu.HBM),
        pltpu.with_memory_space_constraint(tile_values, pltpu.HBM),
    )
    gathered = exchange(degree_part, "col")

    partials, degree_piece = pl.pallas_call(
        functools.partial(first_kernel, halves),
        out_shape=(
            jax.ShapeDtypeStruct((halves * rows, channels, width), jnp.float32),
            jax.ShapeDtypeStruct((1, width), jnp.float32),
        ),
        in_specs=[in_smem(), in_smem(), in_vmem(), in_vmem(), in_vmem()],
        out_specs=(in_vmem(), in_vmem()),
        scratch_shapes=[
            pltpu.VMEM((rows, channels, width), jnp.bfloat16),
            pltpu.VMEM((rows, width), jnp.float32),
        ],
        compiler_params=params,
        name="first",
    )(places, tile_counts, signal, gathered, held)
    received = exchange(partials, "row")
    degree_piece = lax.ppermute(degree_piece, ("row", "col"), to_column)
    walked_piece = 0.5 * jnp.sum(received, axis=0)
    scaled = (walked_piece / degree_piece).astype(jnp.bfloat16)

    column = all_gather(scaled, "row").reshape(halves * rows, channels, width)
    walked_piece = lax.ppermute(walked_piece, ("row", "col"), to_row)
    column, walked_piece = lax.optimization_barrier((column, walked_piece))
    partials = pl.pallas_call(
        second_kernel,
        out_shape=jax.ShapeDtypeStruct((rows, channels, width), jnp.float32),
        in_specs=[in_smem(), in_smem(), in_vmem(), in_vmem()],
        out_specs=in_vmem(),
        compiler_params=params,
        name="second",
    )(places, tile_counts, column, held)
    spread = jnp.sum(exchange(partials, "col"), axis=0)
    lowpass_piece = 0.5 * (walked_piece + spread)

    both = all_gather(jnp.stack([walked_piece, lowpass_piece]), "col")
    both = both.reshape(rows, 2, channels, width)
    return pl.pallas_call(
        output_kernel,
        out_shape=(jax.ShapeDtypeStruct((channels, row_len), jnp.float32),) * 3,
        in_specs=[in_vmem(), in_vmem()],
        out_specs=(in_vmem(),) * 3,
        compiler_params=params,
        name="outputs",
    )(signal, both)


def solution(mesh):
    in_specs = (
        P(None, "row"),
        P("row", "col", None, None, None),
        P("row", "col", None, None),
        P("row", "col"),
    )
    out_specs = (P(None, "row"), P(None, "row"), P(None, "row"))
    return jax.shard_map(
        on_device, mesh=mesh, in_specs=in_specs, out_specs=out_specs, check_vma=False
    )
```

```python
import functools

import jax
import jax.numpy as jnp
from jax import lax
from jax.experimental import pallas as pl
from jax.experimental.pallas import tpu as pltpu
from jax.sharding import PartitionSpec as P

CHUNKS = 8
VMEM_BYTES = 12 * 1024 * 1024


def exchange(partials, axis):
    return lax.all_to_all(partials, axis, 0, 0, tiled=True)


def all_gather(piece, axis):
    return exchange(jnp.broadcast_to(piece[None], (lax.axis_size(axis),) + piece.shape), axis)


def place(places, which, slot):
    return places[0, 0, which, slot]


def degree_kernel(counts, places_hbm, tiles, held, out, places, sums, small, sems):
    slot_count = tiles.shape[2]
    copy_places = pltpu.make_async_copy(places_hbm, places, small)
    copy_places.start()
    step = slot_count // CHUNKS
    copies = []
    for chunk in range(CHUNKS):
        span = pl.ds(chunk * step, step)
        copies.append(pltpu.make_async_copy(tiles.at[0, 0, span], held.at[span], sems.at[chunk]))
        copies[-1].start()
    targets, rows, width = out.shape
    sums[...] = jnp.zeros_like(sums)
    ones = jnp.ones((8, width), jnp.bfloat16)
    copy_places.wait()
    for chunk in range(CHUNKS):
        copies[chunk].wait()
        block = held[chunk * step : (chunk + 1) * step].reshape(step * width, width)
        found = lax.dot_general(
            ones, block, (((1,), (1,)), ((), ())), preferred_element_type=jnp.float32
        )
        for index in range(step):
            slot = chunk * step + index
            row = jnp.where(slot < counts[0, 0], place(places, 0, slot), rows)
            sums[row] += found[:, index * width : (index + 1) * width]
    for row in range(rows):
        for target in range(targets):
            out[target, row : row + 1, :] = sums[row, 0:1, :]


def first_kernel(halves, places, counts, signal, gathered, held, out, piece, scaled, degree):
    slot_count, width, _ = held.shape
    rows = gathered.shape[1]
    row_index = lax.axis_index("row")
    col_index = lax.axis_index("col")
    total = gathered[0]
    for source in range(1, gathered.shape[0]):
        total += gathered[source]
    degree[...] = total
    piece[...] = degree[pl.ds(col_index, 1), :]
    for tile in range(rows):
        block = signal[:, tile * width : (tile + 1) * width]
        scaled[tile] = (block / degree[tile : tile + 1, :]).astype(jnp.bfloat16)
        for half in range(halves):
            own = row_index == col_index * halves + half
            out[half * rows + tile] = jnp.where(own, block, 0.0)
    for slot in range(slot_count):
        left = scaled[place(places, 0, slot)]
        left = jnp.where(slot < counts[0, 0], left, jnp.zeros_like(left))
        target = place(places, 1, slot)
        out[target] += lax.dot_general(
            left, held[slot], (((1,), (0,)), ((), ())), preferred_element_type=jnp.float32
        )


def second_kernel(places, counts, column, held, out):
    for tile in range(out.shape[0]):
        out[tile] = jnp.zeros(out.shape[1:], jnp.float32)
    for slot in range(held.shape[0]):
        left = column[place(places, 1, slot)]
        left = jnp.where(slot < counts[0, 0], left, jnp.zeros_like(left))
        target = place(places, 0, slot)
        out[target] += lax.dot_general(
            left, held[slot], (((1,), (1,)), ((), ())), preferred_element_type=jnp.float32
        )


def output_kernel(signal, both, first, second, low):
    rows, _, _, width = both.shape
    for tile in range(rows):
        span = slice(tile * width, (tile + 1) * width)
        walked = both[tile, 0]
        lowpass = both[tile, 1]
        first[:, span] = jnp.abs(signal[:, span] - walked)
        second[:, span] = jnp.abs(walked - lowpass)
        low[:, span] = lowpass


def in_vmem():
    return pl.BlockSpec(memory_space=pltpu.VMEM)


def in_smem():
    return pl.BlockSpec(memory_space=pltpu.SMEM)


def on_device(signal, tile_values, tile_places, tile_counts):
    channels, row_len = signal.shape
    slot_count, width = tile_values.shape[2:4]
    rows = row_len // width
    row_size = lax.axis_size("row")
    col_size = lax.axis_size("col")
    halves = row_size // col_size
    params = pltpu.CompilerParams(vmem_limit_bytes=VMEM_BYTES)
    to_column = [
        (row * col_size + col, ((row % halves) * rows + col) * col_size + row // halves)
        for row in range(row_size)
        for col in range(col_size)
    ]
    to_row = [(target, source) for source, target in to_column]

    held, degree_part, places = pl.pallas_call(
        degree_kernel,
        out_shape=(
            pltpu.VMEM((slot_count, width, width), jnp.bfloat16),
            jax.ShapeDtypeStruct((col_size, rows, width), jnp.float32),
            pltpu.SMEM(tile_places.shape, jnp.int32),
        ),
        in_specs=[in_smem()] + [pl.BlockSpec(memory_space=pltpu.HBM)] * 2,
        out_specs=(in_vmem(), in_vmem(), in_smem()),
        scratch_shapes=[
            pltpu.VMEM((rows + 1, 8, width), jnp.float32),
            pltpu.SemaphoreType.DMA,
            pltpu.SemaphoreType.DMA((CHUNKS,)),
        ],
        compiler_params=params,
        name="degree",
    )(
        tile_counts,
        pltpu.with_memory_space_constraint(tile_places, pltpu.HBM),
        pltpu.with_memory_space_constraint(tile_values, pltpu.HBM),
    )
    gathered = exchange(degree_part, "col")

    partials, degree_piece = pl.pallas_call(
        functools.partial(first_kernel, halves),
        out_shape=(
            jax.ShapeDtypeStruct((halves * rows, channels, width), jnp.float32),
            jax.ShapeDtypeStruct((1, width), jnp.float32),
        ),
        in_specs=[in_smem(), in_smem(), in_vmem(), in_vmem(), in_vmem()],
        out_specs=(in_vmem(), in_vmem()),
        scratch_shapes=[
            pltpu.VMEM((rows, channels, width), jnp.bfloat16),
            pltpu.VMEM((rows, width), jnp.float32),
        ],
        compiler_params=params,
        name="first",
    )(places, tile_counts, signal, gathered, held)
    received = exchange(partials, "row")
    degree_piece = lax.ppermute(degree_piece, ("row", "col"), to_column)
    walked_piece = 0.5 * jnp.sum(received, axis=0)
    scaled = (walked_piece / degree_piece).astype(jnp.bfloat16)

    column = all_gather(scaled, "row").reshape(halves * rows, channels, width)
    walked_piece = lax.ppermute(walked_piece, ("row", "col"), to_row)
    partials = pl.pallas_call(
        second_kernel,
        out_shape=jax.ShapeDtypeStruct((rows, channels, width), jnp.float32),
        in_specs=[in_smem(), in_smem(), in_vmem(), in_vmem()],
        out_specs=in_vmem(),
        compiler_params=params,
        name="second",
    )(places, tile_counts, column, held)
    partials, walked_piece = lax.optimization_barrier((partials, walked_piece))
    spread = jnp.sum(exchange(partials, "col"), axis=0)
    lowpass_piece = 0.5 * (walked_piece + spread)

    both = all_gather(jnp.stack([walked_piece, lowpass_piece]), "col")
    both = both.reshape(rows, 2, channels, width)
    return pl.pallas_call(
        output_kernel,
        out_shape=(jax.ShapeDtypeStruct((channels, row_len), jnp.float32),) * 3,
        in_specs=[in_vmem(), in_vmem()],
        out_specs=(in_vmem(),) * 3,
        compiler_params=params,
        name="outputs",
    )(signal, both)


def solution(mesh):
    in_specs = (
        P(None, "row"),
        P("row", "col", None, None, None),
        P("row", "col", None, None),
        P("row", "col"),
    )
    out_specs = (P(None, "row"), P(None, "row"), P(None, "row"))
    return jax.shard_map(
        on_device, mesh=mesh, in_specs=in_specs, out_specs=out_specs, check_vma=False
    )
```

```python
import functools

import jax
import jax.numpy as jnp
from jax import lax
from jax.experimental import pallas as pl
from jax.experimental.pallas import tpu as pltpu
from jax.sharding import PartitionSpec as P

CHUNKS = 8
PARTS = 4
VMEM_BYTES = 12 * 1024 * 1024


def exchange(partials, axis):
    return lax.all_to_all(partials, axis, 0, 0, tiled=True)


def all_gather(piece, axis):
    return exchange(jnp.broadcast_to(piece[None], (lax.axis_size(axis),) + piece.shape), axis)


def place(places, which, slot):
    return places[0, 0, which, slot]


def degree_kernel(counts, places_hbm, tiles, held, out, places, sums, small, sems):
    slot_count = tiles.shape[2]
    copy_places = pltpu.make_async_copy(places_hbm, places, small)
    copy_places.start()
    step = slot_count // CHUNKS
    copies = []
    for chunk in range(CHUNKS):
        span = pl.ds(chunk * step, step)
        copies.append(pltpu.make_async_copy(tiles.at[0, 0, span], held.at[span], sems.at[chunk]))
        copies[-1].start()
    targets, rows, width = out.shape
    sums[...] = jnp.zeros_like(sums)
    ones = jnp.ones((8, width), jnp.bfloat16)
    copy_places.wait()
    for chunk in range(CHUNKS):
        copies[chunk].wait()
        block = held[chunk * step : (chunk + 1) * step].reshape(step * width, width)
        found = lax.dot_general(
            ones, block, (((1,), (1,)), ((), ())), preferred_element_type=jnp.float32
        )
        for index in range(step):
            slot = chunk * step + index
            row = jnp.where(slot < counts[0, 0], place(places, 0, slot), rows)
            sums[row] += found[:, index * width : (index + 1) * width]
    for row in range(rows):
        out[0, row : row + 1, :] = sums[row, 0:1, :]
    total = out[0]
    for target in range(1, targets):
        out[target] = total


def first_kernel(halves, places, counts, signal, gathered, held, out, piece, scaled, degree):
    slot_count, width, _ = held.shape
    rows = gathered.shape[1]
    row_index = lax.axis_index("row")
    col_index = lax.axis_index("col")
    total = gathered[0]
    for source in range(1, gathered.shape[0]):
        total += gathered[source]
    degree[...] = total
    piece[...] = degree[pl.ds(col_index, 1), :]
    for tile in range(rows):
        block = signal[:, tile * width : (tile + 1) * width]
        scaled[tile] = (block / degree[tile : tile + 1, :]).astype(jnp.bfloat16)
        for half in range(halves):
            own = row_index == col_index * halves + half
            out[half * rows + tile] = jnp.where(own, block, 0.0)
    for slot in range(slot_count):
        left = scaled[place(places, 0, slot)]
        left = jnp.where(slot < counts[0, 0], left, jnp.zeros_like(left))
        target = place(places, 1, slot)
        out[target] += lax.dot_general(
            left, held[slot], (((1,), (0,)), ((), ())), preferred_element_type=jnp.float32
        )


def second_kernel(places, counts, column, held, out):
    for tile in range(out.shape[0]):
        out[tile] = jnp.zeros(out.shape[1:], jnp.float32)
    for slot in range(held.shape[0]):
        left = column[place(places, 1, slot)]
        left = jnp.where(slot < counts[0, 0], left, jnp.zeros_like(left))
        target = place(places, 0, slot)
        out[target] += lax.dot_general(
            left, held[slot], (((1,), (1,)), ((), ())), preferred_element_type=jnp.float32
        )


def middle_kernel(received, degree, walked, copies):
    total = received[0]
    for source in range(1, received.shape[0]):
        total += received[source]
    total = 0.5 * total
    walked[...] = total
    scaled = (total / degree[...]).astype(jnp.bfloat16)
    for target in range(copies.shape[0]):
        copies[target] = scaled


def output_kernel(signal, both, first, second, low, held, sems):
    rows, _, _, width = both.shape
    step = rows // PARTS
    copies = []
    for part in range(PARTS):
        for tile in range(part * step, (part + 1) * step):
            span = slice(tile * width, (tile + 1) * width)
            walked = both[tile, 0]
            lowpass = both[tile, 1]
            held[0, :, span] = jnp.abs(signal[:, span] - walked)
            held[1, :, span] = jnp.abs(walked - lowpass)
            held[2, :, span] = lowpass
        span = pl.ds(part * step * width, step * width)
        for index, target in enumerate((first, second, low)):
            copies.append(
                pltpu.make_async_copy(held.at[index, :, span], target.at[:, span], sems.at[part, index])
            )
            copies[-1].start()
    for copy in copies:
        copy.wait()


def in_vmem():
    return pl.BlockSpec(memory_space=pltpu.VMEM)


def in_smem():
    return pl.BlockSpec(memory_space=pltpu.SMEM)


def on_device(signal, tile_values, tile_places, tile_counts):
    channels, row_len = signal.shape
    slot_count, width = tile_values.shape[2:4]
    rows = row_len // width
    row_size = lax.axis_size("row")
    col_size = lax.axis_size("col")
    halves = row_size // col_size
    params = pltpu.CompilerParams(vmem_limit_bytes=VMEM_BYTES)
    to_column = [
        (row * col_size + col, ((row % halves) * rows + col) * col_size + row // halves)
        for row in range(row_size)
        for col in range(col_size)
    ]
    to_row = [(target, source) for source, target in to_column]

    held, degree_part, places = pl.pallas_call(
        degree_kernel,
        out_shape=(
            pltpu.VMEM((slot_count, width, width), jnp.bfloat16),
            jax.ShapeDtypeStruct((col_size, rows, width), jnp.float32),
            pltpu.SMEM(tile_places.shape, jnp.int32),
        ),
        in_specs=[in_smem()] + [pl.BlockSpec(memory_space=pltpu.HBM)] * 2,
        out_specs=(in_vmem(), in_vmem(), in_smem()),
        scratch_shapes=[
            pltpu.VMEM((rows + 1, 8, width), jnp.float32),
            pltpu.SemaphoreType.DMA,
            pltpu.SemaphoreType.DMA((CHUNKS,)),
        ],
        compiler_params=params,
        name="degree",
    )(
        tile_counts,
        pltpu.with_memory_space_constraint(tile_places, pltpu.HBM),
        pltpu.with_memory_space_constraint(tile_values, pltpu.HBM),
    )
    gathered = exchange(degree_part, "col")

    partials, degree_piece = pl.pallas_call(
        functools.partial(first_kernel, halves),
        out_shape=(
            jax.ShapeDtypeStruct((halves * rows, channels, width), jnp.float32),
            jax.ShapeDtypeStruct((1, width), jnp.float32),
        ),
        in_specs=[in_smem(), in_smem(), in_vmem(), in_vmem(), in_vmem()],
        out_specs=(in_vmem(), in_vmem()),
        scratch_shapes=[
            pltpu.VMEM((rows, channels, width), jnp.bfloat16),
            pltpu.VMEM((rows, width), jnp.float32),
        ],
        compiler_params=params,
        name="first",
    )(places, tile_counts, signal, gathered, held)
    received = exchange(partials, "row")
    degree_piece = lax.ppermute(degree_piece, ("row", "col"), to_column)
    walked_piece, scaled = pl.pallas_call(
        middle_kernel,
        out_shape=(
            jax.ShapeDtypeStruct((channels, width), jnp.float32),
            jax.ShapeDtypeStruct((row_size, channels, width), jnp.bfloat16),
        ),
        in_specs=[in_vmem(), in_vmem()],
        out_specs=(in_vmem(), in_vmem()),
        compiler_params=params,
        name="middle",
    )(received, degree_piece)

    column = exchange(scaled, "row")
    walked_piece = lax.ppermute(walked_piece, ("row", "col"), to_row)
    partials = pl.pallas_call(
        second_kernel,
        out_shape=jax.ShapeDtypeStruct((rows, channels, width), jnp.float32),
        in_specs=[in_smem(), in_smem(), in_vmem(), in_vmem()],
        out_specs=in_vmem(),
        compiler_params=params,
        name="second",
    )(places, tile_counts, column, held)
    partials, walked_piece = lax.optimization_barrier((partials, walked_piece))
    spread = jnp.sum(exchange(partials, "col"), axis=0)
    lowpass_piece = 0.5 * (walked_piece + spread)

    both = all_gather(jnp.stack([walked_piece, lowpass_piece]), "col")
    both = both.reshape(rows, 2, channels, width)
    return pl.pallas_call(
        output_kernel,
        out_shape=(jax.ShapeDtypeStruct((channels, row_len), jnp.float32),) * 3,
        in_specs=[in_vmem(), in_vmem()],
        out_specs=(pl.BlockSpec(memory_space=pltpu.HBM),) * 3,
        scratch_shapes=[
            pltpu.VMEM((3, channels, row_len), jnp.float32),
            pltpu.SemaphoreType.DMA((PARTS, 3)),
        ],
        compiler_params=params,
        name="outputs",
    )(signal, both)


def solution(mesh):
    in_specs = (
        P(None, "row"),
        P("row", "col", None, None, None),
        P("row", "col", None, None),
        P("row", "col"),
    )
    out_specs = (P(None, "row"), P(None, "row"), P(None, "row"))
    return jax.shard_map(
        on_device, mesh=mesh, in_specs=in_specs, out_specs=out_specs, check_vma=False
    )
```

```python
import functools

import jax
import jax.numpy as jnp
from jax import lax
from jax.experimental import pallas as pl
from jax.experimental.pallas import tpu as pltpu
from jax.sharding import PartitionSpec as P

CHUNKS = 8
VMEM_BYTES = 12 * 1024 * 1024


def exchange(partials, axis):
    return lax.all_to_all(partials, axis, 0, 0, tiled=True)


def all_gather(piece, axis):
    return exchange(jnp.broadcast_to(piece[None], (lax.axis_size(axis),) + piece.shape), axis)


def place(places, which, slot):
    return places[0, 0, which, slot]


def degree_kernel(counts, places_hbm, tiles, held, out, places, sums, small, sems):
    slot_count = tiles.shape[2]
    copy_places = pltpu.make_async_copy(places_hbm, places, small)
    copy_places.start()
    step = slot_count // CHUNKS
    copies = []
    for chunk in range(CHUNKS):
        span = pl.ds(chunk * step, step)
        copies.append(pltpu.make_async_copy(tiles.at[0, 0, span], held.at[span], sems.at[chunk]))
        copies[-1].start()
    targets, rows, width = out.shape
    sums[...] = jnp.zeros_like(sums)
    ones = jnp.ones((8, width), jnp.bfloat16)
    copy_places.wait()
    for chunk in range(CHUNKS):
        copies[chunk].wait()
        block = held[chunk * step : (chunk + 1) * step].reshape(step * width, width)
        found = lax.dot_general(
            ones, block, (((1,), (1,)), ((), ())), preferred_element_type=jnp.float32
        )
        for index in range(step):
            slot = chunk * step + index
            row = jnp.where(slot < counts[0, 0], place(places, 0, slot), rows)
            sums[row] += found[:, index * width : (index + 1) * width]
    for row in range(rows):
        for target in range(targets):
            out[target, row : row + 1, :] = sums[row, 0:1, :]


def first_kernel(halves, places, counts, signal, gathered, held, out, scaled, degree, sums):
    slot_count, width, _ = held.shape
    rows = gathered.shape[1]
    channels = signal.shape[0]
    row_index = lax.axis_index("row")
    col_index = lax.axis_index("col")
    total = gathered[0]
    for source in range(1, gathered.shape[0]):
        total += gathered[source]
    degree[...] = total
    for tile in range(rows):
        block = signal[:, tile * width : (tile + 1) * width]
        nodes = degree[tile : tile + 1, :]
        scaled[tile] = (block / nodes).astype(jnp.bfloat16)
        for half in range(halves):
            own = row_index == col_index * halves + half
            sums[half * rows + tile] = jnp.where(own, block, 0.0)
            out[half * rows + tile, channels] = jnp.where(own, nodes, 0.0)
    for slot in range(slot_count):
        left = scaled[place(places, 0, slot)]
        left = jnp.where(slot < counts[0, 0], left, jnp.zeros_like(left))
        target = place(places, 1, slot)
        sums[target] += lax.dot_general(
            left, held[slot], (((1,), (0,)), ((), ())), preferred_element_type=jnp.float32
        )
    for tile in range(halves * rows):
        for channel in range(channels):
            out[tile, channel] = sums[tile, channel : channel + 1, :]


def middle_kernel(received, walked, copies):
    sources, channels = received.shape[0], received.shape[1] - 1

    def summed(channel):
        total = received[0, channel]
        for source in range(1, sources):
            total += received[source, channel]
        return total

    for channel in range(channels):
        walked[channel : channel + 1, :] = 0.5 * summed(channel)
    scaled = (walked[...] / summed(channels)).astype(jnp.bfloat16)
    for target in range(copies.shape[0]):
        copies[target] = scaled


def second_kernel(places, counts, column, held, out):
    for tile in range(out.shape[0]):
        out[tile] = jnp.zeros(out.shape[1:], jnp.float32)
    for slot in range(held.shape[0]):
        left = column[place(places, 1, slot)]
        left = jnp.where(slot < counts[0, 0], left, jnp.zeros_like(left))
        target = place(places, 0, slot)
        out[target] += lax.dot_general(
            left, held[slot], (((1,), (1,)), ((), ())), preferred_element_type=jnp.float32
        )


def output_kernel(signal, both, first, second, low):
    rows, _, _, width = both.shape
    for tile in range(rows):
        span = slice(tile * width, (tile + 1) * width)
        walked = both[tile, 0]
        lowpass = both[tile, 1]
        first[:, span] = jnp.abs(signal[:, span] - walked)
        second[:, span] = jnp.abs(walked - lowpass)
        low[:, span] = lowpass


def in_vmem():
    return pl.BlockSpec(memory_space=pltpu.VMEM)


def in_smem():
    return pl.BlockSpec(memory_space=pltpu.SMEM)


def on_device(signal, tile_values, tile_places, tile_counts):
    channels, row_len = signal.shape
    slot_count, width = tile_values.shape[2:4]
    rows = row_len // width
    row_size = lax.axis_size("row")
    col_size = lax.axis_size("col")
    halves = row_size // col_size
    params = pltpu.CompilerParams(vmem_limit_bytes=VMEM_BYTES)
    to_row = [
        (((row % halves) * rows + col) * col_size + row // halves, row * col_size + col)
        for row in range(row_size)
        for col in range(col_size)
    ]

    held, degree_part, places = pl.pallas_call(
        degree_kernel,
        out_shape=(
            pltpu.VMEM((slot_count, width, width), jnp.bfloat16),
            jax.ShapeDtypeStruct((col_size, rows, width), jnp.float32),
            pltpu.SMEM(tile_places.shape, jnp.int32),
        ),
        in_specs=[in_smem()] + [pl.BlockSpec(memory_space=pltpu.HBM)] * 2,
        out_specs=(in_vmem(), in_vmem(), in_smem()),
        scratch_shapes=[
            pltpu.VMEM((rows + 1, 8, width), jnp.float32),
            pltpu.SemaphoreType.DMA,
            pltpu.SemaphoreType.DMA((CHUNKS,)),
        ],
        compiler_params=params,
        name="degree",
    )(
        tile_counts,
        pltpu.with_memory_space_constraint(tile_places, pltpu.HBM),
        pltpu.with_memory_space_constraint(tile_values, pltpu.HBM),
    )
    gathered = exchange(degree_part, "col")

    partials = pl.pallas_call(
        functools.partial(first_kernel, halves),
        out_shape=jax.ShapeDtypeStruct((halves * rows, channels + 1, 1, width), jnp.float32),
        in_specs=[in_smem(), in_smem(), in_vmem(), in_vmem(), in_vmem()],
        out_specs=in_vmem(),
        scratch_shapes=[
            pltpu.VMEM((rows, channels, width), jnp.bfloat16),
            pltpu.VMEM((rows, width), jnp.float32),
            pltpu.VMEM((halves * rows, channels, width), jnp.float32),
        ],
        compiler_params=params,
        name="first",
    )(places, tile_counts, signal, gathered, held)
    walked_piece, scaled = pl.pallas_call(
        middle_kernel,
        out_shape=(
            jax.ShapeDtypeStruct((channels, width), jnp.float32),
            jax.ShapeDtypeStruct((row_size, channels, width), jnp.bfloat16),
        ),
        in_specs=[in_vmem()],
        out_specs=(in_vmem(), in_vmem()),
        compiler_params=params,
        name="middle",
    )(exchange(partials, "row"))

    column = exchange(scaled, "row")
    walked_piece = lax.ppermute(walked_piece, ("row", "col"), to_row)
    partials = pl.pallas_call(
        second_kernel,
        out_shape=jax.ShapeDtypeStruct((rows, channels, width), jnp.float32),
        in_specs=[in_smem(), in_smem(), in_vmem(), in_vmem()],
        out_specs=in_vmem(),
        compiler_params=params,
        name="second",
    )(places, tile_counts, column, held)
    partials, walked_piece = lax.optimization_barrier((partials, walked_piece))
    spread = jnp.sum(exchange(partials, "col"), axis=0)
    lowpass_piece = 0.5 * (walked_piece + spread)

    both = all_gather(jnp.stack([walked_piece, lowpass_piece]), "col")
    both = both.reshape(rows, 2, channels, width)
    return pl.pallas_call(
        output_kernel,
        out_shape=(jax.ShapeDtypeStruct((channels, row_len), jnp.float32),) * 3,
        in_specs=[in_vmem(), in_vmem()],
        out_specs=(in_vmem(),) * 3,
        compiler_params=params,
        name="outputs",
    )(signal, both)


def solution(mesh):
    in_specs = (
        P(None, "row"),
        P("row", "col", None, None, None),
        P("row", "col", None, None),
        P("row", "col"),
    )
    out_specs = (P(None, "row"), P(None, "row"), P(None, "row"))
    return jax.shard_map(
        on_device, mesh=mesh, in_specs=in_specs, out_specs=out_specs, check_vma=False
    )
```

```python
import functools

import jax
import jax.numpy as jnp
from jax import lax
from jax.experimental import pallas as pl
from jax.experimental.pallas import tpu as pltpu
from jax.sharding import Mesh, PartitionSpec as P

CHUNKS = 8
CORES = 2
COL = ("chip", "core")
VMEM_BYTES = 12 * 1024 * 1024


def exchange(partials, axis):
    return lax.all_to_all(partials, axis, 0, 0, tiled=True)


def all_gather(piece, axis):
    return exchange(jnp.broadcast_to(piece[None], (lax.axis_size(axis),) + piece.shape), axis)


def place(places, which, slot):
    return places[0, 0, which, slot]


def degree_kernel(counts, places_hbm, tiles, held, out, places, sums, small, sems):
    slot_count = tiles.shape[2]
    copy_places = pltpu.make_async_copy(places_hbm, places, small)
    copy_places.start()
    step = slot_count // CHUNKS
    copies = []
    for chunk in range(CHUNKS):
        span = pl.ds(chunk * step, step)
        copies.append(pltpu.make_async_copy(tiles.at[0, 0, span], held.at[span], sems.at[chunk]))
        copies[-1].start()
    targets, rows, width = out.shape
    sums[...] = jnp.zeros_like(sums)
    ones = jnp.ones((8, width), jnp.bfloat16)
    copy_places.wait()
    for chunk in range(CHUNKS):
        copies[chunk].wait()
        block = held[chunk * step : (chunk + 1) * step].reshape(step * width, width)
        found = lax.dot_general(
            ones, block, (((1,), (1,)), ((), ())), preferred_element_type=jnp.float32
        )
        for index in range(step):
            slot = chunk * step + index
            row = jnp.where(slot < counts[0, 0], place(places, 0, slot), rows)
            sums[row] += found[:, index * width : (index + 1) * width]
    for row in range(rows):
        for target in range(targets):
            out[target, row : row + 1, :] = sums[row, 0:1, :]


def first_kernel(halves, places, counts, signal, gathered, held, out, scaled, degree, sums):
    slot_count, width, _ = held.shape
    rows = gathered.shape[1]
    channels = signal.shape[0]
    row_index = lax.axis_index("row")
    col_index = lax.axis_index("chip") * CORES + lax.axis_index("core")
    total = gathered[0]
    for source in range(1, gathered.shape[0]):
        total += gathered[source]
    degree[...] = total
    for tile in range(rows):
        block = signal[:, tile * width : (tile + 1) * width]
        nodes = degree[tile : tile + 1, :]
        scaled[tile] = (block / nodes).astype(jnp.bfloat16)
        for half in range(halves):
            own = row_index == col_index * halves + half
            sums[half * rows + tile] = jnp.where(own, block, 0.0)
            out[half * rows + tile, channels] = jnp.where(own, nodes, 0.0)
    for slot in range(slot_count):
        left = scaled[place(places, 0, slot)]
        left = jnp.where(slot < counts[0, 0], left, jnp.zeros_like(left))
        target = place(places, 1, slot)
        sums[target] += lax.dot_general(
            left, held[slot], (((1,), (0,)), ((), ())), preferred_element_type=jnp.float32
        )
    for tile in range(halves * rows):
        for channel in range(channels):
            out[tile, channel] = sums[tile, channel : channel + 1, :]


def middle_kernel(received, walked, copies):
    sources, channels = received.shape[0], received.shape[1] - 1

    def summed(channel):
        total = received[0, channel]
        for source in range(1, sources):
            total += received[source, channel]
        return total

    for channel in range(channels):
        walked[channel : channel + 1, :] = 0.5 * summed(channel)
    scaled = (walked[...] / summed(channels)).astype(jnp.bfloat16)
    for target in range(copies.shape[0]):
        copies[target] = scaled


def second_kernel(places, counts, column, held, out):
    for tile in range(out.shape[0]):
        out[tile] = jnp.zeros(out.shape[1:], jnp.float32)
    for slot in range(held.shape[0]):
        left = column[place(places, 1, slot)]
        left = jnp.where(slot < counts[0, 0], left, jnp.zeros_like(left))
        target = place(places, 0, slot)
        out[target] += lax.dot_general(
            left, held[slot], (((1,), (1,)), ((), ())), preferred_element_type=jnp.float32
        )


def output_kernel(signal, both, first, second, low):
    cores, chips, _, _, width = both.shape
    for tile in range(chips * cores):
        span = slice(tile * width, (tile + 1) * width)
        walked = both[tile % cores, tile // cores, 0]
        lowpass = both[tile % cores, tile // cores, 1]
        first[:, span] = jnp.abs(signal[:, span] - walked)
        second[:, span] = jnp.abs(walked - lowpass)
        low[:, span] = lowpass


def in_vmem():
    return pl.BlockSpec(memory_space=pltpu.VMEM)


def in_smem():
    return pl.BlockSpec(memory_space=pltpu.SMEM)


def on_device(signal, tile_values, tile_places, tile_counts):
    channels, row_len = signal.shape
    slot_count, width = tile_values.shape[2:4]
    rows = row_len // width
    row_size = lax.axis_size("row")
    col_size = lax.axis_size(COL)
    halves = row_size // col_size
    params = pltpu.CompilerParams(vmem_limit_bytes=VMEM_BYTES)
    to_row = [
        (((row % halves) * rows + col) * col_size + row // halves, row * col_size + col)
        for row in range(row_size)
        for col in range(col_size)
    ]

    held, degree_part, places = pl.pallas_call(
        degree_kernel,
        out_shape=(
            pltpu.VMEM((slot_count, width, width), jnp.bfloat16),
            jax.ShapeDtypeStruct((col_size, rows, width), jnp.float32),
            pltpu.SMEM(tile_places.shape, jnp.int32),
        ),
        in_specs=[in_smem()] + [pl.BlockSpec(memory_space=pltpu.HBM)] * 2,
        out_specs=(in_vmem(), in_vmem(), in_smem()),
        scratch_shapes=[
            pltpu.VMEM((rows + 1, 8, width), jnp.float32),
            pltpu.SemaphoreType.DMA,
            pltpu.SemaphoreType.DMA((CHUNKS,)),
        ],
        compiler_params=params,
        name="degree",
    )(
        tile_counts,
        pltpu.with_memory_space_constraint(tile_places, pltpu.HBM),
        pltpu.with_memory_space_constraint(tile_values, pltpu.HBM),
    )
    gathered = exchange(degree_part, COL)

    partials = pl.pallas_call(
        functools.partial(first_kernel, halves),
        out_shape=jax.ShapeDtypeStruct((halves * rows, channels + 1, 1, width), jnp.float32),
        in_specs=[in_smem(), in_smem(), in_vmem(), in_vmem(), in_vmem()],
        out_specs=in_vmem(),
        scratch_shapes=[
            pltpu.VMEM((rows, channels, width), jnp.bfloat16),
            pltpu.VMEM((rows, width), jnp.float32),
            pltpu.VMEM((halves * rows, channels, width), jnp.float32),
        ],
        compiler_params=params,
        name="first",
    )(places, tile_counts, signal, gathered, held)
    walked_piece, scaled = pl.pallas_call(
        middle_kernel,
        out_shape=(
            jax.ShapeDtypeStruct((channels, width), jnp.float32),
            jax.ShapeDtypeStruct((row_size, channels, width), jnp.bfloat16),
        ),
        in_specs=[in_vmem()],
        out_specs=(in_vmem(), in_vmem()),
        compiler_params=params,
        name="middle",
    )(exchange(partials, "row"))

    column = exchange(scaled, "row")
    walked_piece = lax.ppermute(walked_piece, ("row",) + COL, to_row)
    partials = pl.pallas_call(
        second_kernel,
        out_shape=jax.ShapeDtypeStruct((rows, channels, width), jnp.float32),
        in_specs=[in_smem(), in_smem(), in_vmem(), in_vmem()],
        out_specs=in_vmem(),
        compiler_params=params,
        name="second",
    )(places, tile_counts, column, held)
    partials, walked_piece = lax.optimization_barrier((partials, walked_piece))
    spread = jnp.sum(exchange(partials, COL), axis=0)
    lowpass_piece = 0.5 * (walked_piece + spread)

    both = all_gather(jnp.stack([walked_piece, lowpass_piece]), "chip")
    both = lax.all_gather(both, "core")
    return pl.pallas_call(
        output_kernel,
        out_shape=(jax.ShapeDtypeStruct((channels, row_len), jnp.float32),) * 3,
        in_specs=[in_vmem(), in_vmem()],
        out_specs=(in_vmem(),) * 3,
        compiler_params=params,
        name="outputs",
    )(signal, both)


def solution(mesh):
    row_size, col_size = mesh.devices.shape
    mesh = Mesh(mesh.devices.reshape(row_size, col_size // CORES, CORES), ("row",) + COL)
    in_specs = (
        P(None, "row"),
        P("row", COL, None, None, None),
        P("row", COL, None, None),
        P("row", COL),
    )
    out_specs = (P(None, "row"), P(None, "row"), P(None, "row"))
    return jax.shard_map(
        on_device, mesh=mesh, in_specs=in_specs, out_specs=out_specs, check_vma=False
    )
```

```python
import functools

import jax
import jax.numpy as jnp
from jax import lax
from jax.experimental import pallas as pl
from jax.experimental.pallas import tpu as pltpu
from jax.sharding import Mesh, PartitionSpec as P

CHUNKS = 2
CORES = 2
COL = ("chip", "core")
VMEM_BYTES = 12 * 1024 * 1024


def exchange(partials, axis):
    return lax.all_to_all(partials, axis, 0, 0, tiled=True)


def all_gather(piece, axis):
    return exchange(jnp.broadcast_to(piece[None], (lax.axis_size(axis),) + piece.shape), axis)


def place(places, which, slot):
    return places[0, 0, which, slot]


def degree_kernel(counts, places_hbm, tiles, held, out, places, sums, small, sems):
    slot_count = tiles.shape[2]
    copy_places = pltpu.make_async_copy(places_hbm, places, small)
    copy_places.start()
    step = slot_count // CHUNKS
    copies = []
    for chunk in range(CHUNKS):
        span = pl.ds(chunk * step, step)
        copies.append(pltpu.make_async_copy(tiles.at[0, 0, span], held.at[span], sems.at[chunk]))
        copies[-1].start()
    targets, rows, width = out.shape
    sums[...] = jnp.zeros_like(sums)
    ones = jnp.ones((8, width), jnp.bfloat16)
    copy_places.wait()
    for chunk in range(CHUNKS):
        copies[chunk].wait()
        block = held[chunk * step : (chunk + 1) * step].reshape(step * width, width)
        found = lax.dot_general(
            ones, block, (((1,), (1,)), ((), ())), preferred_element_type=jnp.float32
        )
        for index in range(step):
            slot = chunk * step + index
            row = jnp.where(slot < counts[0, 0], place(places, 0, slot), rows)
            sums[row] += found[:, index * width : (index + 1) * width]
    for row in range(rows):
        for target in range(targets):
            out[target, row : row + 1, :] = sums[row, 0:1, :]


def first_kernel(halves, places, counts, signal, gathered, held, out, scaled, degree, sums):
    slot_count, width, _ = held.shape
    rows = gathered.shape[1]
    channels = signal.shape[0]
    row_index = lax.axis_index("row")
    col_index = lax.axis_index("chip") * CORES + lax.axis_index("core")
    total = gathered[0]
    for source in range(1, gathered.shape[0]):
        total += gathered[source]
    degree[...] = total
    for tile in range(rows):
        block = signal[:, tile * width : (tile + 1) * width]
        nodes = degree[tile : tile + 1, :]
        scaled[tile] = (block / nodes).astype(jnp.bfloat16)
        for half in range(halves):
            own = row_index == col_index * halves + half
            sums[half * rows + tile] = jnp.where(own, block, 0.0)
            end = (half * rows + tile + 1) * (channels + 1)
            out[end - 1 : end, :] = jnp.where(own, nodes, 0.0)
    for slot in range(slot_count):
        left = scaled[place(places, 0, slot)]
        left = jnp.where(slot < counts[0, 0], left, jnp.zeros_like(left))
        target = place(places, 1, slot)
        sums[target] += lax.dot_general(
            left, held[slot], (((1,), (0,)), ((), ())), preferred_element_type=jnp.float32
        )
    for tile in range(halves * rows):
        start = tile * (channels + 1)
        out[start : start + channels, :] = sums[tile]


def middle_kernel(received, walked, copies):
    channels = walked.shape[0]
    sources = received.shape[0] // (channels + 1)
    total, degree = 0.0, 0.0
    for source in range(sources):
        start = source * (channels + 1)
        total += received[start : start + channels, :]
        degree += received[start + channels : start + channels + 1, :]
    total = 0.5 * total
    walked[...] = total
    scaled = (total / degree).astype(jnp.bfloat16)
    for target in range(copies.shape[0]):
        copies[target] = scaled


def second_kernel(places, counts, column, held, out):
    for tile in range(out.shape[0]):
        out[tile] = jnp.zeros(out.shape[1:], jnp.float32)
    for slot in range(held.shape[0]):
        left = column[place(places, 1, slot)]
        left = jnp.where(slot < counts[0, 0], left, jnp.zeros_like(left))
        target = place(places, 0, slot)
        out[target] += lax.dot_general(
            left, held[slot], (((1,), (1,)), ((), ())), preferred_element_type=jnp.float32
        )


def output_kernel(signal, both, first, second, low):
    cores, chips, _, _, width = both.shape
    for tile in range(chips * cores):
        span = slice(tile * width, (tile + 1) * width)
        walked = both[tile % cores, tile // cores, 0]
        lowpass = both[tile % cores, tile // cores, 1]
        first[:, span] = jnp.abs(signal[:, span] - walked)
        second[:, span] = jnp.abs(walked - lowpass)
        low[:, span] = lowpass


def in_vmem():
    return pl.BlockSpec(memory_space=pltpu.VMEM)


def in_smem():
    return pl.BlockSpec(memory_space=pltpu.SMEM)


def on_device(signal, tile_values, tile_places, tile_counts):
    channels, row_len = signal.shape
    slot_count, width = tile_values.shape[2:4]
    rows = row_len // width
    row_size = lax.axis_size("row")
    col_size = lax.axis_size(COL)
    halves = row_size // col_size
    params = pltpu.CompilerParams(vmem_limit_bytes=VMEM_BYTES)
    to_row = [
        (((row % halves) * rows + col) * col_size + row // halves, row * col_size + col)
        for row in range(row_size)
        for col in range(col_size)
    ]

    held, degree_part, places = pl.pallas_call(
        degree_kernel,
        out_shape=(
            pltpu.VMEM((slot_count, width, width), jnp.bfloat16),
            jax.ShapeDtypeStruct((col_size, rows, width), jnp.float32),
            pltpu.SMEM(tile_places.shape, jnp.int32),
        ),
        in_specs=[in_smem()] + [pl.BlockSpec(memory_space=pltpu.HBM)] * 2,
        out_specs=(in_vmem(), in_vmem(), in_smem()),
        scratch_shapes=[
            pltpu.VMEM((rows + 1, 8, width), jnp.float32),
            pltpu.SemaphoreType.DMA,
            pltpu.SemaphoreType.DMA((CHUNKS,)),
        ],
        compiler_params=params,
        name="degree",
    )(
        tile_counts,
        pltpu.with_memory_space_constraint(tile_places, pltpu.HBM),
        pltpu.with_memory_space_constraint(tile_values, pltpu.HBM),
    )
    gathered = exchange(degree_part, COL)

    partials = pl.pallas_call(
        functools.partial(first_kernel, halves),
        out_shape=jax.ShapeDtypeStruct((halves * rows * (channels + 1), width), jnp.float32),
        in_specs=[in_smem(), in_smem(), in_vmem(), in_vmem(), in_vmem()],
        out_specs=in_vmem(),
        scratch_shapes=[
            pltpu.VMEM((rows, channels, width), jnp.bfloat16),
            pltpu.VMEM((rows, width), jnp.float32),
            pltpu.VMEM((halves * rows, channels, width), jnp.float32),
        ],
        compiler_params=params,
        name="first",
    )(places, tile_counts, signal, gathered, held)
    received = exchange(partials.reshape(row_size, channels + 1, 1, width), "row")
    walked_piece, scaled = pl.pallas_call(
        middle_kernel,
        out_shape=(
            jax.ShapeDtypeStruct((channels, width), jnp.float32),
            jax.ShapeDtypeStruct((row_size, channels, width), jnp.bfloat16),
        ),
        in_specs=[in_vmem()],
        out_specs=(in_vmem(), in_vmem()),
        compiler_params=params,
        name="middle",
    )(received.reshape(row_size * (channels + 1), width))

    column = exchange(scaled, "row")
    walked_piece = lax.ppermute(walked_piece, ("row",) + COL, to_row)
    partials = pl.pallas_call(
        second_kernel,
        out_shape=jax.ShapeDtypeStruct((rows, channels, width), jnp.float32),
        in_specs=[in_smem(), in_smem(), in_vmem(), in_vmem()],
        out_specs=in_vmem(),
        compiler_params=params,
        name="second",
    )(places, tile_counts, column, held)
    partials, walked_piece = lax.optimization_barrier((partials, walked_piece))
    spread = jnp.sum(exchange(partials, COL), axis=0)
    lowpass_piece = 0.5 * (walked_piece + spread)

    both = all_gather(jnp.stack([walked_piece, lowpass_piece]), "chip")
    both = lax.all_gather(both, "core")
    return pl.pallas_call(
        output_kernel,
        out_shape=(jax.ShapeDtypeStruct((channels, row_len), jnp.float32),) * 3,
        in_specs=[in_vmem(), in_vmem()],
        out_specs=(in_vmem(),) * 3,
        compiler_params=params,
        name="outputs",
    )(signal, both)


def solution(mesh):
    row_size, col_size = mesh.devices.shape
    mesh = Mesh(mesh.devices.reshape(row_size, col_size // CORES, CORES), ("row",) + COL)
    in_specs = (
        P(None, "row"),
        P("row", COL, None, None, None),
        P("row", COL, None, None),
        P("row", COL),
    )
    out_specs = (P(None, "row"), P(None, "row"), P(None, "row"))
    return jax.shard_map(
        on_device, mesh=mesh, in_specs=in_specs, out_specs=out_specs, check_vma=False
    )
```

```python
import functools

import jax
import jax.numpy as jnp
from jax import lax
from jax.experimental import pallas as pl
from jax.experimental.pallas import tpu as pltpu
from jax.sharding import Mesh, PartitionSpec as P

CHUNKS = 2
CORES = 2
LINES = 4
COL = ("chip", "core")
ROW = ("line", "plane")
VMEM_BYTES = 12 * 1024 * 1024


def exchange(partials, axis):
    return lax.all_to_all(partials, axis, 0, 0, tiled=True)


def all_gather(piece, axis):
    return exchange(jnp.broadcast_to(piece[None], (lax.axis_size(axis),) + piece.shape), axis)


def place(places, which, slot):
    return places[0, 0, which, slot]


def degree_kernel(counts, places_hbm, tiles, held, out, places, sums, small, sems):
    slot_count = tiles.shape[2]
    copy_places = pltpu.make_async_copy(places_hbm, places, small)
    copy_places.start()
    step = slot_count // CHUNKS
    copies = []
    for chunk in range(CHUNKS):
        span = pl.ds(chunk * step, step)
        copies.append(pltpu.make_async_copy(tiles.at[0, 0, span], held.at[span], sems.at[chunk]))
        copies[-1].start()
    targets, rows, width = out.shape
    sums[...] = jnp.zeros_like(sums)
    ones = jnp.ones((8, width), jnp.bfloat16)
    copy_places.wait()
    for chunk in range(CHUNKS):
        copies[chunk].wait()
        block = held[chunk * step : (chunk + 1) * step].reshape(step * width, width)
        found = lax.dot_general(
            ones, block, (((1,), (1,)), ((), ())), preferred_element_type=jnp.float32
        )
        for index in range(step):
            slot = chunk * step + index
            row = jnp.where(slot < counts[0, 0], place(places, 0, slot), rows)
            sums[row] += found[:, index * width : (index + 1) * width]
    for row in range(rows):
        for target in range(targets):
            out[target, row : row + 1, :] = sums[row, 0:1, :]


def first_kernel(halves, places, counts, signal, gathered, held, out, scaled, degree, sums):
    slot_count, width, _ = held.shape
    rows = gathered.shape[1]
    channels = signal.shape[0]
    row_index = lax.axis_index("plane") * LINES + lax.axis_index("line")
    col_index = lax.axis_index("chip") * CORES + lax.axis_index("core")
    total = gathered[0]
    for source in range(1, gathered.shape[0]):
        total += gathered[source]
    degree[...] = total
    for tile in range(rows):
        block = signal[:, tile * width : (tile + 1) * width]
        nodes = degree[tile : tile + 1, :]
        scaled[tile] = (block / nodes).astype(jnp.bfloat16)
        for half in range(halves):
            own = row_index == col_index * halves + half
            sums[half * rows + tile] = jnp.where(own, block, 0.0)
            end = (half * rows + tile + 1) * (channels + 1)
            out[end - 1 : end, :] = jnp.where(own, nodes, 0.0)
    for slot in range(slot_count):
        left = scaled[place(places, 0, slot)]
        left = jnp.where(slot < counts[0, 0], left, jnp.zeros_like(left))
        target = place(places, 1, slot)
        sums[target] += lax.dot_general(
            left, held[slot], (((1,), (0,)), ((), ())), preferred_element_type=jnp.float32
        )
    for tile in range(halves * rows):
        start = tile * (channels + 1)
        out[start : start + channels, :] = sums[tile]


def middle_kernel(received, walked, copies):
    channels = walked.shape[0]
    sources = received.shape[0] // (channels + 1)
    total, degree = 0.0, 0.0
    for source in range(sources):
        start = source * (channels + 1)
        total += received[start : start + channels, :]
        degree += received[start + channels : start + channels + 1, :]
    total = 0.5 * total
    walked[...] = total
    scaled = (total / degree).astype(jnp.bfloat16)
    for target in range(copies.shape[0]):
        copies[target] = scaled


def second_kernel(places, counts, column, held, out):
    for tile in range(out.shape[0]):
        out[tile] = jnp.zeros(out.shape[1:], jnp.float32)
    for slot in range(held.shape[0]):
        left = column[place(places, 1, slot)]
        left = jnp.where(slot < counts[0, 0], left, jnp.zeros_like(left))
        target = place(places, 0, slot)
        out[target] += lax.dot_general(
            left, held[slot], (((1,), (1,)), ((), ())), preferred_element_type=jnp.float32
        )


def output_kernel(signal, both, first, second, low):
    cores, chips, _, _, width = both.shape
    for tile in range(chips * cores):
        span = slice(tile * width, (tile + 1) * width)
        walked = both[tile % cores, tile // cores, 0]
        lowpass = both[tile % cores, tile // cores, 1]
        first[:, span] = jnp.abs(signal[:, span] - walked)
        second[:, span] = jnp.abs(walked - lowpass)
        low[:, span] = lowpass


def in_vmem():
    return pl.BlockSpec(memory_space=pltpu.VMEM)


def in_smem():
    return pl.BlockSpec(memory_space=pltpu.SMEM)


def on_device(signal, tile_values, tile_places, tile_counts):
    channels, row_len = signal.shape
    slot_count, width = tile_values.shape[2:4]
    rows = row_len // width
    row_size = lax.axis_size(ROW)
    planes = row_size // LINES
    col_size = lax.axis_size(COL)
    halves = row_size // col_size
    params = pltpu.CompilerParams(vmem_limit_bytes=VMEM_BYTES)
    to_row = []
    for row in range(row_size):
        for col in range(col_size):
            piece = (row % halves) * rows + col
            source = (piece % planes) * LINES + piece // planes
            to_row.append((source * col_size + row // halves, row * col_size + col))

    held, degree_part, places = pl.pallas_call(
        degree_kernel,
        out_shape=(
            pltpu.VMEM((slot_count, width, width), jnp.bfloat16),
            jax.ShapeDtypeStruct((col_size, rows, width), jnp.float32),
            pltpu.SMEM(tile_places.shape, jnp.int32),
        ),
        in_specs=[in_smem()] + [pl.BlockSpec(memory_space=pltpu.HBM)] * 2,
        out_specs=(in_vmem(), in_vmem(), in_smem()),
        scratch_shapes=[
            pltpu.VMEM((rows + 1, 8, width), jnp.float32),
            pltpu.SemaphoreType.DMA,
            pltpu.SemaphoreType.DMA((CHUNKS,)),
        ],
        compiler_params=params,
        name="degree",
    )(
        tile_counts,
        pltpu.with_memory_space_constraint(tile_places, pltpu.HBM),
        pltpu.with_memory_space_constraint(tile_values, pltpu.HBM),
    )
    gathered = exchange(degree_part, COL)

    partials = pl.pallas_call(
        functools.partial(first_kernel, halves),
        out_shape=jax.ShapeDtypeStruct((halves * rows * (channels + 1), width), jnp.float32),
        in_specs=[in_smem(), in_smem(), in_vmem(), in_vmem(), in_vmem()],
        out_specs=in_vmem(),
        scratch_shapes=[
            pltpu.VMEM((rows, channels, width), jnp.bfloat16),
            pltpu.VMEM((rows, width), jnp.float32),
            pltpu.VMEM((halves * rows, channels, width), jnp.float32),
        ],
        compiler_params=params,
        name="first",
    )(places, tile_counts, signal, gathered, held)
    received = exchange(partials.reshape(row_size, channels + 1, 1, width), ROW)
    walked_piece, scaled = pl.pallas_call(
        middle_kernel,
        out_shape=(
            jax.ShapeDtypeStruct((channels, width), jnp.float32),
            jax.ShapeDtypeStruct((row_size, channels, width), jnp.bfloat16),
        ),
        in_specs=[in_vmem()],
        out_specs=(in_vmem(), in_vmem()),
        compiler_params=params,
        name="middle",
    )(received.reshape(row_size * (channels + 1), width))

    column = exchange(scaled, ROW)
    walked_piece = lax.ppermute(walked_piece, ("plane", "line") + COL, to_row)
    partials = pl.pallas_call(
        second_kernel,
        out_shape=jax.ShapeDtypeStruct((rows, channels, width), jnp.float32),
        in_specs=[in_smem(), in_smem(), in_vmem(), in_vmem()],
        out_specs=in_vmem(),
        compiler_params=params,
        name="second",
    )(places, tile_counts, column, held)
    partials, walked_piece = lax.optimization_barrier((partials, walked_piece))
    spread = jnp.sum(exchange(partials, COL), axis=0)
    lowpass_piece = 0.5 * (walked_piece + spread)

    both = all_gather(jnp.stack([walked_piece, lowpass_piece]), "chip")
    both = lax.all_gather(both, "core")
    return pl.pallas_call(
        output_kernel,
        out_shape=(jax.ShapeDtypeStruct((channels, row_len), jnp.float32),) * 3,
        in_specs=[in_vmem(), in_vmem()],
        out_specs=(in_vmem(),) * 3,
        compiler_params=params,
        name="outputs",
    )(signal, both)


def solution(mesh):
    row_size, col_size = mesh.devices.shape
    shape = (row_size // LINES, LINES, col_size // CORES, CORES)
    mesh = Mesh(mesh.devices.reshape(shape), ("plane", "line") + COL)
    rows = ("plane", "line")
    in_specs = (
        P(None, rows),
        P(rows, COL, None, None, None),
        P(rows, COL, None, None),
        P(rows, COL),
    )
    out_specs = (P(None, rows), P(None, rows), P(None, rows))
    return jax.shard_map(
        on_device, mesh=mesh, in_specs=in_specs, out_specs=out_specs, check_vma=False
    )
```

```python
import functools

import jax
import jax.numpy as jnp
from jax import lax
from jax.experimental import pallas as pl
from jax.experimental.pallas import tpu as pltpu
from jax.sharding import Mesh, PartitionSpec as P

CHUNKS = 2
CORES = 2
LINES = 4
COL = ("chip", "core")
ROW = ("line", "plane")
VMEM_BYTES = 12 * 1024 * 1024


def exchange(partials, axis):
    return lax.all_to_all(partials, axis, 0, 0, tiled=True)


def all_gather(piece, axis):
    return exchange(jnp.broadcast_to(piece[None], (lax.axis_size(axis),) + piece.shape), axis)


def place(places, which, slot):
    return places[0, 0, which, slot]


def degree_kernel(counts, places_hbm, tiles, held, out, places, sums, small, sems):
    slot_count = tiles.shape[2]
    copy_places = pltpu.make_async_copy(places_hbm, places, small)
    copy_places.start()
    step = slot_count // CHUNKS
    copies = []
    for chunk in range(CHUNKS):
        span = pl.ds(chunk * step, step)
        copies.append(pltpu.make_async_copy(tiles.at[0, 0, span], held.at[span], sems.at[chunk]))
        copies[-1].start()
    targets, rows, width = out.shape
    sums[...] = jnp.zeros_like(sums)
    ones = jnp.ones((8, width), jnp.bfloat16)
    copy_places.wait()
    for chunk in range(CHUNKS):
        copies[chunk].wait()
        block = held[chunk * step : (chunk + 1) * step].reshape(step * width, width)
        found = lax.dot_general(
            ones, block, (((1,), (1,)), ((), ())), preferred_element_type=jnp.float32
        )
        for index in range(step):
            slot = chunk * step + index
            row = jnp.where(slot < counts[0, 0], place(places, 0, slot), rows)
            sums[row] += found[:, index * width : (index + 1) * width]
    for row in range(rows):
        for target in range(targets):
            out[target, row : row + 1, :] = sums[row, 0:1, :]


def first_kernel(halves, places, counts, signal, gathered, held, out, scaled, degree, sums):
    slot_count, width, _ = held.shape
    rows = gathered.shape[1]
    channels = signal.shape[0]
    row_index = lax.axis_index("plane") * LINES + lax.axis_index("line")
    col_index = lax.axis_index("chip") * CORES + lax.axis_index("core")
    total = gathered[0]
    for source in range(1, gathered.shape[0]):
        total += gathered[source]
    degree[...] = total
    for tile in range(rows):
        block = signal[:, tile * width : (tile + 1) * width]
        nodes = degree[tile : tile + 1, :]
        scaled[tile] = (block / nodes).astype(jnp.bfloat16)
        for half in range(halves):
            own = row_index == col_index * halves + half
            sums[half * rows + tile] = jnp.where(own, block, 0.0)
            end = (half * rows + tile + 1) * (channels + 1)
            out[end - 1 : end, :] = jnp.where(own, nodes, 0.0)
    for slot in range(slot_count):
        left = scaled[place(places, 0, slot)]
        left = jnp.where(slot < counts[0, 0], left, jnp.zeros_like(left))
        target = place(places, 1, slot)
        sums[target] += lax.dot_general(
            left, held[slot], (((1,), (0,)), ((), ())), preferred_element_type=jnp.float32
        )
    for tile in range(halves * rows):
        start = tile * (channels + 1)
        out[start : start + channels, :] = sums[tile]


def middle_kernel(received, walked, copies):
    channels = walked.shape[0]
    sources = received.shape[0] // (channels + 1)
    total, degree = 0.0, 0.0
    for source in range(sources):
        start = source * (channels + 1)
        total += received[start : start + channels, :]
        degree += received[start + channels : start + channels + 1, :]
    total = 0.5 * total
    walked[...] = total
    scaled = (total / degree).astype(jnp.bfloat16)
    for target in range(copies.shape[0]):
        copies[target] = scaled


def flip_kernel(held, out):
    for slot in range(held.shape[0]):
        out[slot] = held[slot].T


def second_kernel(places, counts, column, flipped, out):
    for tile in range(out.shape[0]):
        out[tile] = jnp.zeros(out.shape[1:], jnp.float32)
    for slot in range(flipped.shape[0]):
        left = column[place(places, 1, slot)]
        left = jnp.where(slot < counts[0, 0], left, jnp.zeros_like(left))
        target = place(places, 0, slot)
        out[target] += lax.dot_general(
            left, flipped[slot], (((1,), (0,)), ((), ())), preferred_element_type=jnp.float32
        )


def output_kernel(signal, both, first, second, low):
    cores, chips, _, _, width = both.shape
    for tile in range(chips * cores):
        span = slice(tile * width, (tile + 1) * width)
        walked = both[tile % cores, tile // cores, 0]
        lowpass = both[tile % cores, tile // cores, 1]
        first[:, span] = jnp.abs(signal[:, span] - walked)
        second[:, span] = jnp.abs(walked - lowpass)
        low[:, span] = lowpass


def in_vmem():
    return pl.BlockSpec(memory_space=pltpu.VMEM)


def in_smem():
    return pl.BlockSpec(memory_space=pltpu.SMEM)


def on_device(signal, tile_values, tile_places, tile_counts):
    channels, row_len = signal.shape
    slot_count, width = tile_values.shape[2:4]
    rows = row_len // width
    row_size = lax.axis_size(ROW)
    planes = row_size // LINES
    col_size = lax.axis_size(COL)
    halves = row_size // col_size
    params = pltpu.CompilerParams(vmem_limit_bytes=VMEM_BYTES)
    to_row = []
    for row in range(row_size):
        for col in range(col_size):
            piece = (row % halves) * rows + col
            source = (piece % planes) * LINES + piece // planes
            to_row.append((source * col_size + row // halves, row * col_size + col))

    held, degree_part, places = pl.pallas_call(
        degree_kernel,
        out_shape=(
            pltpu.VMEM((slot_count, width, width), jnp.bfloat16),
            jax.ShapeDtypeStruct((col_size, rows, width), jnp.float32),
            pltpu.SMEM(tile_places.shape, jnp.int32),
        ),
        in_specs=[in_smem()] + [pl.BlockSpec(memory_space=pltpu.HBM)] * 2,
        out_specs=(in_vmem(), in_vmem(), in_smem()),
        scratch_shapes=[
            pltpu.VMEM((rows + 1, 8, width), jnp.float32),
            pltpu.SemaphoreType.DMA,
            pltpu.SemaphoreType.DMA((CHUNKS,)),
        ],
        compiler_params=params,
        name="degree",
    )(
        tile_counts,
        pltpu.with_memory_space_constraint(tile_places, pltpu.HBM),
        pltpu.with_memory_space_constraint(tile_values, pltpu.HBM),
    )
    gathered = exchange(degree_part, COL)

    partials = pl.pallas_call(
        functools.partial(first_kernel, halves),
        out_shape=jax.ShapeDtypeStruct((halves * rows * (channels + 1), width), jnp.float32),
        in_specs=[in_smem(), in_smem(), in_vmem(), in_vmem(), in_vmem()],
        out_specs=in_vmem(),
        scratch_shapes=[
            pltpu.VMEM((rows, channels, width), jnp.bfloat16),
            pltpu.VMEM((rows, width), jnp.float32),
            pltpu.VMEM((halves * rows, channels, width), jnp.float32),
        ],
        compiler_params=params,
        name="first",
    )(places, tile_counts, signal, gathered, held)
    received = exchange(partials.reshape(row_size, channels + 1, 1, width), ROW)
    walked_piece, scaled = pl.pallas_call(
        middle_kernel,
        out_shape=(
            jax.ShapeDtypeStruct((channels, width), jnp.float32),
            jax.ShapeDtypeStruct((row_size, channels, width), jnp.bfloat16),
        ),
        in_specs=[in_vmem()],
        out_specs=(in_vmem(), in_vmem()),
        compiler_params=params,
        name="middle",
    )(received.reshape(row_size * (channels + 1), width))

    scaled, held = lax.optimization_barrier((scaled, held))
    flipped = pl.pallas_call(
        flip_kernel,
        out_shape=pltpu.VMEM(held.shape, held.dtype),
        in_specs=[in_vmem()],
        out_specs=in_vmem(),
        input_output_aliases={0: 0},
        compiler_params=params,
        name="flip",
    )(held)
    column = exchange(scaled, ROW)
    walked_piece = lax.ppermute(walked_piece, ("plane", "line") + COL, to_row)
    partials = pl.pallas_call(
        second_kernel,
        out_shape=jax.ShapeDtypeStruct((rows, channels, width), jnp.float32),
        in_specs=[in_smem(), in_smem(), in_vmem(), in_vmem()],
        out_specs=in_vmem(),
        compiler_params=params,
        name="second",
    )(places, tile_counts, column, flipped)
    partials, walked_piece = lax.optimization_barrier((partials, walked_piece))
    spread = jnp.sum(exchange(partials, COL), axis=0)
    lowpass_piece = 0.5 * (walked_piece + spread)

    both = all_gather(jnp.stack([walked_piece, lowpass_piece]), "chip")
    both = lax.all_gather(both, "core")
    return pl.pallas_call(
        output_kernel,
        out_shape=(jax.ShapeDtypeStruct((channels, row_len), jnp.float32),) * 3,
        in_specs=[in_vmem(), in_vmem()],
        out_specs=(in_vmem(),) * 3,
        compiler_params=params,
        name="outputs",
    )(signal, both)


def solution(mesh):
    row_size, col_size = mesh.devices.shape
    shape = (row_size // LINES, LINES, col_size // CORES, CORES)
    mesh = Mesh(mesh.devices.reshape(shape), ("plane", "line") + COL)
    rows = ("plane", "line")
    in_specs = (
        P(None, rows),
        P(rows, COL, None, None, None),
        P(rows, COL, None, None),
        P(rows, COL),
    )
    out_specs = (P(None, rows), P(None, rows), P(None, rows))
    return jax.shard_map(
        on_device, mesh=mesh, in_specs=in_specs, out_specs=out_specs, check_vma=False
    )
```

```python
import functools

import jax
import jax.numpy as jnp
from jax import lax
from jax.experimental import pallas as pl
from jax.experimental.pallas import tpu as pltpu
from jax.sharding import Mesh, PartitionSpec as P

CHUNKS = 2
BATCH = 4
CORES = 2
LINES = 4
COL = ("chip", "core")
ROW = ("line", "plane")
VMEM_BYTES = 12 * 1024 * 1024


def exchange(partials, axis):
    return lax.all_to_all(partials, axis, 0, 0, tiled=True)


def all_gather(piece, axis):
    return exchange(jnp.broadcast_to(piece[None], (lax.axis_size(axis),) + piece.shape), axis)


def place(places, which, slot):
    return places[0, 0, which, slot]


def degree_kernel(counts, places_hbm, tiles, held, out, places, sums, small, sems):
    slot_count = tiles.shape[2]
    copy_places = pltpu.make_async_copy(places_hbm, places, small)
    copy_places.start()
    step = slot_count // CHUNKS
    copies = []
    for chunk in range(CHUNKS):
        span = pl.ds(chunk * step, step)
        copies.append(pltpu.make_async_copy(tiles.at[0, 0, span], held.at[span], sems.at[chunk]))
        copies[-1].start()
    targets, rows, width = out.shape
    sums[...] = jnp.zeros_like(sums)
    ones = jnp.ones((8, width), jnp.bfloat16)
    copy_places.wait()
    for chunk in range(CHUNKS):
        copies[chunk].wait()
        block = held[chunk * step : (chunk + 1) * step].reshape(step * width, width)
        found = lax.dot_general(
            ones, block, (((1,), (1,)), ((), ())), preferred_element_type=jnp.float32
        )
        for index in range(step):
            slot = chunk * step + index
            row = jnp.where(slot < counts[0, 0], place(places, 0, slot), rows)
            sums[row] += found[:, index * width : (index + 1) * width]
    for row in range(rows):
        for target in range(targets):
            out[target, row : row + 1, :] = sums[row, 0:1, :]


def first_kernel(halves, places, counts, signal, gathered, held, out, scaled, degree, sums):
    slot_count, width, _ = held.shape
    rows = gathered.shape[1]
    channels = signal.shape[0]
    row_index = lax.axis_index("plane") * LINES + lax.axis_index("line")
    col_index = lax.axis_index("chip") * CORES + lax.axis_index("core")
    total = gathered[0]
    for source in range(1, gathered.shape[0]):
        total += gathered[source]
    degree[...] = total
    for tile in range(rows):
        block = signal[:, tile * width : (tile + 1) * width]
        nodes = degree[tile : tile + 1, :]
        scaled[tile] = (block / nodes).astype(jnp.bfloat16)
        for half in range(halves):
            own = row_index == col_index * halves + half
            sums[half * rows + tile] = jnp.where(own, block, 0.0)
            end = (half * rows + tile + 1) * (channels + 1)
            out[end - 1 : end, :] = jnp.where(own, nodes, 0.0)
    for slot in range(slot_count):
        left = scaled[place(places, 0, slot)]
        left = jnp.where(slot < counts[0, 0], left, jnp.zeros_like(left))
        target = place(places, 1, slot)
        sums[target] += lax.dot_general(
            left, held[slot], (((1,), (0,)), ((), ())), preferred_element_type=jnp.float32
        )
    for tile in range(halves * rows):
        start = tile * (channels + 1)
        out[start : start + channels, :] = sums[tile]


def middle_kernel(received, walked, copies):
    channels = walked.shape[0]
    sources = received.shape[0] // (channels + 1)
    total, degree = 0.0, 0.0
    for source in range(sources):
        start = source * (channels + 1)
        total += received[start : start + channels, :]
        degree += received[start + channels : start + channels + 1, :]
    total = 0.5 * total
    walked[...] = total
    scaled = (total / degree).astype(jnp.bfloat16)
    for target in range(copies.shape[0]):
        copies[target] = scaled


def flip_kernel(held, out):
    for start in range(0, held.shape[0], BATCH):
        tiles = [held[slot].T for slot in range(start, start + BATCH)]
        for index, tile in enumerate(tiles):
            out[start + index] = tile


def second_kernel(places, counts, column, flipped, out):
    for tile in range(out.shape[0]):
        out[tile] = jnp.zeros(out.shape[1:], jnp.float32)
    for slot in range(flipped.shape[0]):
        left = column[place(places, 1, slot)]
        left = jnp.where(slot < counts[0, 0], left, jnp.zeros_like(left))
        target = place(places, 0, slot)
        out[target] += lax.dot_general(
            left, flipped[slot], (((1,), (0,)), ((), ())), preferred_element_type=jnp.float32
        )


def output_kernel(signal, both, first, second, low):
    cores, chips, _, _, width = both.shape
    for tile in range(chips * cores):
        span = slice(tile * width, (tile + 1) * width)
        walked = both[tile % cores, tile // cores, 0]
        lowpass = both[tile % cores, tile // cores, 1]
        first[:, span] = jnp.abs(signal[:, span] - walked)
        second[:, span] = jnp.abs(walked - lowpass)
        low[:, span] = lowpass


def in_vmem():
    return pl.BlockSpec(memory_space=pltpu.VMEM)


def in_smem():
    return pl.BlockSpec(memory_space=pltpu.SMEM)


def on_device(signal, tile_values, tile_places, tile_counts):
    channels, row_len = signal.shape
    slot_count, width = tile_values.shape[2:4]
    rows = row_len // width
    row_size = lax.axis_size(ROW)
    planes = row_size // LINES
    col_size = lax.axis_size(COL)
    halves = row_size // col_size
    params = pltpu.CompilerParams(vmem_limit_bytes=VMEM_BYTES)
    to_row = []
    for row in range(row_size):
        for col in range(col_size):
            piece = (row % halves) * rows + col
            source = (piece % planes) * LINES + piece // planes
            to_row.append((source * col_size + row // halves, row * col_size + col))

    held, degree_part, places = pl.pallas_call(
        degree_kernel,
        out_shape=(
            pltpu.VMEM((slot_count, width, width), jnp.bfloat16),
            jax.ShapeDtypeStruct((col_size, rows, width), jnp.float32),
            pltpu.SMEM(tile_places.shape, jnp.int32),
        ),
        in_specs=[in_smem()] + [pl.BlockSpec(memory_space=pltpu.HBM)] * 2,
        out_specs=(in_vmem(), in_vmem(), in_smem()),
        scratch_shapes=[
            pltpu.VMEM((rows + 1, 8, width), jnp.float32),
            pltpu.SemaphoreType.DMA,
            pltpu.SemaphoreType.DMA((CHUNKS,)),
        ],
        compiler_params=params,
        name="degree",
    )(
        tile_counts,
        pltpu.with_memory_space_constraint(tile_places, pltpu.HBM),
        pltpu.with_memory_space_constraint(tile_values, pltpu.HBM),
    )
    gathered = exchange(degree_part, COL)

    partials = pl.pallas_call(
        functools.partial(first_kernel, halves),
        out_shape=jax.ShapeDtypeStruct((halves * rows * (channels + 1), width), jnp.float32),
        in_specs=[in_smem(), in_smem(), in_vmem(), in_vmem(), in_vmem()],
        out_specs=in_vmem(),
        scratch_shapes=[
            pltpu.VMEM((rows, channels, width), jnp.bfloat16),
            pltpu.VMEM((rows, width), jnp.float32),
            pltpu.VMEM((halves * rows, channels, width), jnp.float32),
        ],
        compiler_params=params,
        name="first",
    )(places, tile_counts, signal, gathered, held)
    received = exchange(partials.reshape(row_size, channels + 1, 1, width), ROW)
    walked_piece, scaled = pl.pallas_call(
        middle_kernel,
        out_shape=(
            jax.ShapeDtypeStruct((channels, width), jnp.float32),
            jax.ShapeDtypeStruct((row_size, channels, width), jnp.bfloat16),
        ),
        in_specs=[in_vmem()],
        out_specs=(in_vmem(), in_vmem()),
        compiler_params=params,
        name="middle",
    )(received.reshape(row_size * (channels + 1), width))

    scaled, held = lax.optimization_barrier((scaled, held))
    flipped = pl.pallas_call(
        flip_kernel,
        out_shape=pltpu.VMEM(held.shape, held.dtype),
        in_specs=[in_vmem()],
        out_specs=in_vmem(),
        input_output_aliases={0: 0},
        compiler_params=params,
        name="flip",
    )(held)
    column = exchange(scaled, ROW)
    walked_piece = lax.ppermute(walked_piece, ("plane", "line") + COL, to_row)
    partials = pl.pallas_call(
        second_kernel,
        out_shape=jax.ShapeDtypeStruct((rows, channels, width), jnp.float32),
        in_specs=[in_smem(), in_smem(), in_vmem(), in_vmem()],
        out_specs=in_vmem(),
        compiler_params=params,
        name="second",
    )(places, tile_counts, column, flipped)
    partials, walked_piece = lax.optimization_barrier((partials, walked_piece))
    spread = jnp.sum(exchange(partials, COL), axis=0)
    lowpass_piece = 0.5 * (walked_piece + spread)

    both = all_gather(jnp.stack([walked_piece, lowpass_piece]), "chip")
    both = lax.all_gather(both, "core")
    return pl.pallas_call(
        output_kernel,
        out_shape=(jax.ShapeDtypeStruct((channels, row_len), jnp.float32),) * 3,
        in_specs=[in_vmem(), in_vmem()],
        out_specs=(in_vmem(),) * 3,
        compiler_params=params,
        name="outputs",
    )(signal, both)


def solution(mesh):
    row_size, col_size = mesh.devices.shape
    shape = (row_size // LINES, LINES, col_size // CORES, CORES)
    mesh = Mesh(mesh.devices.reshape(shape), ("plane", "line") + COL)
    rows = ("plane", "line")
    in_specs = (
        P(None, rows),
        P(rows, COL, None, None, None),
        P(rows, COL, None, None),
        P(rows, COL),
    )
    out_specs = (P(None, rows), P(None, rows), P(None, rows))
    return jax.shard_map(
        on_device, mesh=mesh, in_specs=in_specs, out_specs=out_specs, check_vma=False
    )
```

```python
import functools

import jax
import jax.numpy as jnp
from jax import lax
from jax.experimental import pallas as pl
from jax.experimental.pallas import tpu as pltpu
from jax.sharding import Mesh, PartitionSpec as P

CHUNKS = 2
CORES = 2
LINES = 4
SIDES = 2
CHIP = ("lane", "side")
COL = CHIP + ("core",)
ROW = ("line", "plane")
MESH = ("plane", "line", "side", "lane", "core")
VMEM_BYTES = 12 * 1024 * 1024


def exchange(partials, axis):
    return lax.all_to_all(partials, axis, 0, 0, tiled=True)


def all_gather(piece, axis):
    return exchange(jnp.broadcast_to(piece[None], (lax.axis_size(axis),) + piece.shape), axis)


def place(places, which, slot):
    return places[0, 0, which, slot]


def degree_kernel(counts, places_hbm, tiles, held, out, places, sums, small, sems):
    slot_count = tiles.shape[2]
    copy_places = pltpu.make_async_copy(places_hbm, places, small)
    copy_places.start()
    step = slot_count // CHUNKS
    copies = []
    for chunk in range(CHUNKS):
        span = pl.ds(chunk * step, step)
        copies.append(pltpu.make_async_copy(tiles.at[0, 0, span], held.at[span], sems.at[chunk]))
        copies[-1].start()
    targets, rows, width = out.shape
    sums[...] = jnp.zeros_like(sums)
    ones = jnp.ones((8, width), jnp.bfloat16)
    copy_places.wait()
    for chunk in range(CHUNKS):
        copies[chunk].wait()
        block = held[chunk * step : (chunk + 1) * step].reshape(step * width, width)
        found = lax.dot_general(
            ones, block, (((1,), (1,)), ((), ())), preferred_element_type=jnp.float32
        )
        for index in range(step):
            slot = chunk * step + index
            row = jnp.where(slot < counts[0, 0], place(places, 0, slot), rows)
            sums[row] += found[:, index * width : (index + 1) * width]
    for row in range(rows):
        for target in range(targets):
            out[target, row : row + 1, :] = sums[row, 0:1, :]


def first_kernel(halves, places, counts, signal, gathered, held, out, scaled, degree, sums):
    slot_count, width, _ = held.shape
    rows = gathered.shape[1]
    channels = signal.shape[0]
    row_index = lax.axis_index("plane") * LINES + lax.axis_index("line")
    lanes = lax.axis_size("lane")
    col_index = lax.axis_index("side") * lanes + lax.axis_index("lane")
    col_index = col_index * CORES + lax.axis_index("core")
    total = gathered[0]
    for source in range(1, gathered.shape[0]):
        total += gathered[source]
    degree[...] = total
    for tile in range(rows):
        block = signal[:, tile * width : (tile + 1) * width]
        nodes = degree[tile : tile + 1, :]
        scaled[tile] = (block / nodes).astype(jnp.bfloat16)
        for half in range(halves):
            own = row_index == col_index * halves + half
            sums[half * rows + tile] = jnp.where(own, block, 0.0)
            end = (half * rows + tile + 1) * (channels + 1)
            out[end - 1 : end, :] = jnp.where(own, nodes, 0.0)
    for slot in range(slot_count):
        left = scaled[place(places, 0, slot)]
        left = jnp.where(slot < counts[0, 0], left, jnp.zeros_like(left))
        target = place(places, 1, slot)
        sums[target] += lax.dot_general(
            left, held[slot], (((1,), (0,)), ((), ())), preferred_element_type=jnp.float32
        )
    for tile in range(halves * rows):
        start = tile * (channels + 1)
        out[start : start + channels, :] = sums[tile]


def middle_kernel(received, walked, copies):
    channels = walked.shape[0]
    sources = received.shape[0] // (channels + 1)
    total, degree = 0.0, 0.0
    for source in range(sources):
        start = source * (channels + 1)
        total += received[start : start + channels, :]
        degree += received[start + channels : start + channels + 1, :]
    total = 0.5 * total
    walked[...] = total
    scaled = (total / degree).astype(jnp.bfloat16)
    for target in range(copies.shape[0]):
        copies[target] = scaled


def flip_kernel(held, out):
    for slot in range(held.shape[0]):
        out[slot] = held[slot].T


def second_kernel(places, counts, column, flipped, out):
    for tile in range(out.shape[0]):
        out[tile] = jnp.zeros(out.shape[1:], jnp.float32)
    for slot in range(flipped.shape[0]):
        left = column[place(places, 1, slot)]
        left = jnp.where(slot < counts[0, 0], left, jnp.zeros_like(left))
        target = place(places, 0, slot)
        out[target] += lax.dot_general(
            left, flipped[slot], (((1,), (0,)), ((), ())), preferred_element_type=jnp.float32
        )


def output_kernel(signal, both, first, second, low):
    cores, chips, _, _, width = both.shape
    for tile in range(chips * cores):
        span = slice(tile * width, (tile + 1) * width)
        walked = both[tile % cores, tile // cores, 0]
        lowpass = both[tile % cores, tile // cores, 1]
        first[:, span] = jnp.abs(signal[:, span] - walked)
        second[:, span] = jnp.abs(walked - lowpass)
        low[:, span] = lowpass


def in_vmem():
    return pl.BlockSpec(memory_space=pltpu.VMEM)


def in_smem():
    return pl.BlockSpec(memory_space=pltpu.SMEM)


def on_device(signal, tile_values, tile_places, tile_counts):
    channels, row_len = signal.shape
    slot_count, width = tile_values.shape[2:4]
    rows = row_len // width
    row_size = lax.axis_size(ROW)
    planes = row_size // LINES
    col_size = lax.axis_size(COL)
    halves = row_size // col_size
    params = pltpu.CompilerParams(vmem_limit_bytes=VMEM_BYTES)
    lanes = lax.axis_size("lane")
    to_row = []
    for row in range(row_size):
        for col in range(col_size):
            chip, core = divmod(col, CORES)
            tile = ((chip % lanes) * SIDES + chip // lanes) * CORES + core
            piece = (row % halves) * rows + tile
            source = (piece % planes) * LINES + piece // planes
            to_row.append((source * col_size + row // halves, row * col_size + col))

    held, degree_part, places = pl.pallas_call(
        degree_kernel,
        out_shape=(
            pltpu.VMEM((slot_count, width, width), jnp.bfloat16),
            jax.ShapeDtypeStruct((col_size, rows, width), jnp.float32),
            pltpu.SMEM(tile_places.shape, jnp.int32),
        ),
        in_specs=[in_smem()] + [pl.BlockSpec(memory_space=pltpu.HBM)] * 2,
        out_specs=(in_vmem(), in_vmem(), in_smem()),
        scratch_shapes=[
            pltpu.VMEM((rows + 1, 8, width), jnp.float32),
            pltpu.SemaphoreType.DMA,
            pltpu.SemaphoreType.DMA((CHUNKS,)),
        ],
        compiler_params=params,
        name="degree",
    )(
        tile_counts,
        pltpu.with_memory_space_constraint(tile_places, pltpu.HBM),
        pltpu.with_memory_space_constraint(tile_values, pltpu.HBM),
    )
    gathered = exchange(degree_part, COL)

    partials = pl.pallas_call(
        functools.partial(first_kernel, halves),
        out_shape=jax.ShapeDtypeStruct((halves * rows * (channels + 1), width), jnp.float32),
        in_specs=[in_smem(), in_smem(), in_vmem(), in_vmem(), in_vmem()],
        out_specs=in_vmem(),
        scratch_shapes=[
            pltpu.VMEM((rows, channels, width), jnp.bfloat16),
            pltpu.VMEM((rows, width), jnp.float32),
            pltpu.VMEM((halves * rows, channels, width), jnp.float32),
        ],
        compiler_params=params,
        name="first",
    )(places, tile_counts, signal, gathered, held)
    received = exchange(partials.reshape(row_size, channels + 1, 1, width), ROW)
    walked_piece, scaled = pl.pallas_call(
        middle_kernel,
        out_shape=(
            jax.ShapeDtypeStruct((channels, width), jnp.float32),
            jax.ShapeDtypeStruct((row_size, channels, width), jnp.bfloat16),
        ),
        in_specs=[in_vmem()],
        out_specs=(in_vmem(), in_vmem()),
        compiler_params=params,
        name="middle",
    )(received.reshape(row_size * (channels + 1), width))

    scaled, held = lax.optimization_barrier((scaled, held))
    flipped = pl.pallas_call(
        flip_kernel,
        out_shape=pltpu.VMEM(held.shape, held.dtype),
        in_specs=[in_vmem()],
        out_specs=in_vmem(),
        input_output_aliases={0: 0},
        compiler_params=params,
        name="flip",
    )(held)
    column = exchange(scaled, ROW)
    walked_piece = lax.ppermute(walked_piece, MESH, to_row)
    partials = pl.pallas_call(
        second_kernel,
        out_shape=jax.ShapeDtypeStruct((rows, channels, width), jnp.float32),
        in_specs=[in_smem(), in_smem(), in_vmem(), in_vmem()],
        out_specs=in_vmem(),
        compiler_params=params,
        name="second",
    )(places, tile_counts, column, flipped)
    partials, walked_piece = lax.optimization_barrier((partials, walked_piece))
    spread = jnp.sum(exchange(partials, COL), axis=0)
    lowpass_piece = 0.5 * (walked_piece + spread)

    both = all_gather(jnp.stack([walked_piece, lowpass_piece]), CHIP)
    both = lax.all_gather(both, "core")
    return pl.pallas_call(
        output_kernel,
        out_shape=(jax.ShapeDtypeStruct((channels, row_len), jnp.float32),) * 3,
        in_specs=[in_vmem(), in_vmem()],
        out_specs=(in_vmem(),) * 3,
        compiler_params=params,
        name="outputs",
    )(signal, both)


def solution(mesh):
    row_size, col_size = mesh.devices.shape
    shape = (row_size // LINES, LINES, SIDES, col_size // (SIDES * CORES), CORES)
    mesh = Mesh(mesh.devices.reshape(shape), MESH)
    rows, cols = MESH[:2], MESH[2:]
    in_specs = (
        P(None, rows),
        P(rows, cols, None, None, None),
        P(rows, cols, None, None),
        P(rows, cols),
    )
    out_specs = (P(None, rows), P(None, rows), P(None, rows))
    return jax.shard_map(
        on_device, mesh=mesh, in_specs=in_specs, out_specs=out_specs, check_vma=False
    )
```

```python
import functools

import jax
import jax.numpy as jnp
from jax import lax
from jax.experimental import pallas as pl
from jax.experimental.pallas import tpu as pltpu
from jax.sharding import Mesh, PartitionSpec as P

CHUNKS = 2
CORES = 2
LINES = 4
COL = ("chip", "core")
ROW = ("line", "plane")
VMEM_BYTES = 12 * 1024 * 1024


def exchange(partials, axis):
    return lax.all_to_all(partials, axis, 0, 0, tiled=True)


def all_gather(piece, axis):
    return exchange(jnp.broadcast_to(piece[None], (lax.axis_size(axis),) + piece.shape), axis)


def place(places, which, slot):
    return places[0, 0, which, slot]


def degree_kernel(counts, places_hbm, tiles, held, out, places, sums, small, sems):
    slot_count = tiles.shape[2]
    copy_places = pltpu.make_async_copy(places_hbm, places, small)
    copy_places.start()
    step = slot_count // CHUNKS
    copies = []
    for chunk in range(CHUNKS):
        span = pl.ds(chunk * step, step)
        copies.append(pltpu.make_async_copy(tiles.at[0, 0, span], held.at[span], sems.at[chunk]))
        copies[-1].start()
    targets, rows, width = out.shape
    sums[...] = jnp.zeros_like(sums)
    ones = jnp.ones((8, width), jnp.bfloat16)
    copy_places.wait()
    for chunk in range(CHUNKS):
        copies[chunk].wait()
        block = held[chunk * step : (chunk + 1) * step].reshape(step * width, width)
        found = lax.dot_general(
            ones, block, (((1,), (1,)), ((), ())), preferred_element_type=jnp.float32
        )
        for index in range(step):
            slot = chunk * step + index
            row = jnp.where(slot < counts[0, 0], place(places, 0, slot), rows)
            sums[row] += found[:, index * width : (index + 1) * width]
    for row in range(rows):
        for target in range(targets):
            out[target, row : row + 1, :] = sums[row, 0:1, :]


def first_kernel(halves, places, counts, signal, gathered, held, out, scaled, degree, sums):
    slot_count, width, _ = held.shape
    rows = gathered.shape[1]
    channels = signal.shape[0]
    row_index = lax.axis_index("plane") * LINES + lax.axis_index("line")
    col_index = lax.axis_index("chip") * CORES + lax.axis_index("core")
    total = gathered[0]
    for source in range(1, gathered.shape[0]):
        total += gathered[source]
    degree[...] = total
    for tile in range(rows):
        block = signal[:, tile * width : (tile + 1) * width]
        nodes = degree[tile : tile + 1, :]
        scaled[tile] = (block / nodes).astype(jnp.bfloat16)
        for half in range(halves):
            own = row_index == col_index * halves + half
            sums[half * rows + tile] = jnp.where(own, block, 0.0)
            end = (half * rows + tile + 1) * (channels + 1)
            out[end - 1 : end, :] = jnp.where(own, nodes, 0.0)
    for slot in range(slot_count):
        left = scaled[place(places, 0, slot)]
        left = jnp.where(slot < counts[0, 0], left, jnp.zeros_like(left))
        target = place(places, 1, slot)
        sums[target] += lax.dot_general(
            left, held[slot], (((1,), (0,)), ((), ())), preferred_element_type=jnp.float32
        )
    for tile in range(halves * rows):
        start = tile * (channels + 1)
        out[start : start + channels, :] = sums[tile]


def middle_kernel(received, walked, copies):
    channels = walked.shape[0]
    sources = received.shape[0] // (channels + 1)
    total, degree = 0.0, 0.0
    for source in range(sources):
        start = source * (channels + 1)
        total += received[start : start + channels, :]
        degree += received[start + channels : start + channels + 1, :]
    total = 0.5 * total
    walked[...] = total
    scaled = (total / degree).astype(jnp.bfloat16)
    for target in range(copies.shape[0]):
        copies[target] = scaled


def flip_kernel(held, out):
    for slot in range(held.shape[0]):
        out[slot] = held[slot].T


def second_kernel(places, counts, column, flipped, out):
    for tile in range(out.shape[0]):
        out[tile] = jnp.zeros(out.shape[1:], jnp.float32)
    for slot in range(flipped.shape[0]):
        left = column[place(places, 1, slot)]
        left = jnp.where(slot < counts[0, 0], left, jnp.zeros_like(left))
        target = place(places, 0, slot)
        out[target] += lax.dot_general(
            left, flipped[slot], (((1,), (0,)), ((), ())), preferred_element_type=jnp.float32
        )


def output_kernel(signal, both, first, second, low):
    cores, chips, _, _, width = both.shape
    for tile in range(chips * cores):
        span = slice(tile * width, (tile + 1) * width)
        walked = both[tile % cores, tile // cores, 0]
        lowpass = both[tile % cores, tile // cores, 1]
        first[:, span] = jnp.abs(signal[:, span] - walked)
        second[:, span] = jnp.abs(walked - lowpass)
        low[:, span] = lowpass


def in_vmem():
    return pl.BlockSpec(memory_space=pltpu.VMEM)


def in_smem():
    return pl.BlockSpec(memory_space=pltpu.SMEM)


def on_device(signal, tile_values, tile_places, tile_counts):
    channels, row_len = signal.shape
    slot_count, width = tile_values.shape[2:4]
    rows = row_len // width
    row_size = lax.axis_size(ROW)
    planes = row_size // LINES
    col_size = lax.axis_size(COL)
    halves = row_size // col_size
    params = pltpu.CompilerParams(vmem_limit_bytes=VMEM_BYTES)
    to_row = []
    for row in range(row_size):
        for col in range(col_size):
            piece = (row % halves) * rows + col
            source = (piece % planes) * LINES + piece // planes
            to_row.append((source * col_size + row // halves, row * col_size + col))

    held, degree_part, places = pl.pallas_call(
        degree_kernel,
        out_shape=(
            pltpu.VMEM((slot_count, width, width), jnp.bfloat16),
            jax.ShapeDtypeStruct((col_size, rows, width), jnp.float32),
            pltpu.SMEM(tile_places.shape, jnp.int32),
        ),
        in_specs=[in_smem()] + [pl.BlockSpec(memory_space=pltpu.HBM)] * 2,
        out_specs=(in_vmem(), in_vmem(), in_smem()),
        scratch_shapes=[
            pltpu.VMEM((rows + 1, 8, width), jnp.float32),
            pltpu.SemaphoreType.DMA,
            pltpu.SemaphoreType.DMA((CHUNKS,)),
        ],
        compiler_params=params,
        name="degree",
    )(
        tile_counts,
        pltpu.with_memory_space_constraint(tile_places, pltpu.HBM),
        pltpu.with_memory_space_constraint(tile_values, pltpu.HBM),
    )
    gathered = exchange(degree_part, COL)

    partials = pl.pallas_call(
        functools.partial(first_kernel, halves),
        out_shape=jax.ShapeDtypeStruct((halves * rows * (channels + 1), width), jnp.float32),
        in_specs=[in_smem(), in_smem(), in_vmem(), in_vmem(), in_vmem()],
        out_specs=in_vmem(),
        scratch_shapes=[
            pltpu.VMEM((rows, channels, width), jnp.bfloat16),
            pltpu.VMEM((rows, width), jnp.float32),
            pltpu.VMEM((halves * rows, channels, width), jnp.float32),
        ],
        compiler_params=params,
        name="first",
    )(places, tile_counts, signal, gathered, held)
    received = exchange(partials.reshape(row_size, channels + 1, 1, width), ROW)
    walked_piece, scaled = pl.pallas_call(
        middle_kernel,
        out_shape=(
            jax.ShapeDtypeStruct((channels, width), jnp.float32),
            jax.ShapeDtypeStruct((row_size, channels, width), jnp.bfloat16),
        ),
        in_specs=[in_vmem()],
        out_specs=(in_vmem(), in_vmem()),
        compiler_params=params,
        name="middle",
    )(received.reshape(row_size * (channels + 1), width))

    scaled, held = lax.optimization_barrier((scaled, held))
    flipped = pl.pallas_call(
        flip_kernel,
        out_shape=pltpu.VMEM(held.shape, held.dtype),
        in_specs=[in_vmem()],
        out_specs=in_vmem(),
        input_output_aliases={0: 0},
        compiler_params=params,
        name="flip",
    )(held)
    column = exchange(scaled, ROW)
    flipped, walked_piece = lax.optimization_barrier((flipped, walked_piece))
    walked_piece = lax.ppermute(walked_piece, ("plane", "line") + COL, to_row)
    partials = pl.pallas_call(
        second_kernel,
        out_shape=jax.ShapeDtypeStruct((rows, channels, width), jnp.float32),
        in_specs=[in_smem(), in_smem(), in_vmem(), in_vmem()],
        out_specs=in_vmem(),
        compiler_params=params,
        name="second",
    )(places, tile_counts, column, flipped)
    partials, walked_piece = lax.optimization_barrier((partials, walked_piece))
    spread = jnp.sum(exchange(partials, COL), axis=0)
    lowpass_piece = 0.5 * (walked_piece + spread)

    both = all_gather(jnp.stack([walked_piece, lowpass_piece]), "chip")
    both = lax.all_gather(both, "core")
    return pl.pallas_call(
        output_kernel,
        out_shape=(jax.ShapeDtypeStruct((channels, row_len), jnp.float32),) * 3,
        in_specs=[in_vmem(), in_vmem()],
        out_specs=(in_vmem(),) * 3,
        compiler_params=params,
        name="outputs",
    )(signal, both)


def solution(mesh):
    row_size, col_size = mesh.devices.shape
    shape = (row_size // LINES, LINES, col_size // CORES, CORES)
    mesh = Mesh(mesh.devices.reshape(shape), ("plane", "line") + COL)
    rows = ("plane", "line")
    in_specs = (
        P(None, rows),
        P(rows, COL, None, None, None),
        P(rows, COL, None, None),
        P(rows, COL),
    )
    out_specs = (P(None, rows), P(None, rows), P(None, rows))
    return jax.shard_map(
        on_device, mesh=mesh, in_specs=in_specs, out_specs=out_specs, check_vma=False
    )
```

```python
import functools

import jax
import jax.numpy as jnp
from jax import lax
from jax.experimental import pallas as pl
from jax.experimental.pallas import tpu as pltpu
from jax.sharding import Mesh, PartitionSpec as P

CHUNKS = 2
CORES = 2
LINES = 4
COL = ("chip", "core")
ROW = ("line", "plane")
VMEM_BYTES = 12 * 1024 * 1024


def exchange(partials, axis):
    return lax.all_to_all(partials, axis, 0, 0, tiled=True)


def all_gather(piece, axis):
    return exchange(jnp.broadcast_to(piece[None], (lax.axis_size(axis),) + piece.shape), axis)


def place(places, which, slot):
    return places[0, 0, which, slot]


def keeper(tile, rows, planes):
    half, tile = tile // rows, tile % rows
    return (2 * (tile // planes) + 1 - half) * planes + tile % planes


def degree_kernel(planes, counts, places_hbm, tiles, held, out, places, sums, small, sems):
    slot_count = tiles.shape[2]
    copy_places = pltpu.make_async_copy(places_hbm, places, small)
    copy_places.start()
    step = slot_count // CHUNKS
    copies = []
    for chunk in range(CHUNKS):
        span = pl.ds(chunk * step, step)
        copies.append(pltpu.make_async_copy(tiles.at[0, 0, span], held.at[span], sems.at[chunk]))
        copies[-1].start()
    targets, rows, width = out.shape
    sums[...] = jnp.zeros_like(sums)
    ones = jnp.ones((8, width), jnp.bfloat16)
    copy_places.wait()
    for chunk in range(CHUNKS):
        copies[chunk].wait()
        block = held[chunk * step : (chunk + 1) * step].reshape(step * width, width)
        found = lax.dot_general(
            ones, block, (((1,), (1,)), ((), ())), preferred_element_type=jnp.float32
        )
        for index in range(step):
            slot = chunk * step + index
            row = jnp.where(slot < counts[0, 0], place(places, 0, slot), rows)
            tile = place(places, 1, slot)
            half = jnp.where(tile < rows, 0, 1)
            tile = tile - half * rows
            upper = jnp.where(tile < planes, 0, 1)
            places[0, 0, 1, slot] = (upper + 1 - half) * planes + tile
            sums[row] += found[:, index * width : (index + 1) * width]
    for row in range(rows):
        for target in range(targets):
            out[target, row : row + 1, :] = sums[row, 0:1, :]


def first_kernel(halves, places, counts, signal, gathered, held, out, scaled, degree, sums):
    slot_count, width, _ = held.shape
    rows = gathered.shape[1]
    channels = signal.shape[0]
    row_index = lax.axis_index("plane") * LINES + lax.axis_index("line")
    col_index = lax.axis_index("chip") * CORES + lax.axis_index("core")
    total = gathered[0]
    for source in range(1, gathered.shape[0]):
        total += gathered[source]
    degree[...] = total
    for tile in range(rows):
        block = signal[:, tile * width : (tile + 1) * width]
        nodes = degree[tile : tile + 1, :]
        scaled[tile] = (block / nodes).astype(jnp.bfloat16)
        for half in range(halves):
            own = row_index == col_index * halves + half
            piece = keeper(half * rows + tile, rows, out.shape[0] // (channels + 1) // LINES)
            sums[piece] = jnp.where(own, block, 0.0)
            end = (piece + 1) * (channels + 1)
            out[end - 1 : end, :] = jnp.where(own, nodes, 0.0)
    for slot in range(slot_count):
        left = scaled[place(places, 0, slot)]
        left = jnp.where(slot < counts[0, 0], left, jnp.zeros_like(left))
        target = place(places, 1, slot)
        sums[target] += lax.dot_general(
            left, held[slot], (((1,), (0,)), ((), ())), preferred_element_type=jnp.float32
        )
    for tile in range(halves * rows):
        start = tile * (channels + 1)
        out[start : start + channels, :] = sums[tile]


def middle_kernel(received, walked, copies):
    channels = walked.shape[0]
    sources = received.shape[0] // (channels + 1)
    total, degree = 0.0, 0.0
    for source in range(sources):
        start = source * (channels + 1)
        total += received[start : start + channels, :]
        degree += received[start + channels : start + channels + 1, :]
    total = 0.5 * total
    walked[...] = total
    scaled = (total / degree).astype(jnp.bfloat16)
    for target in range(copies.shape[0]):
        copies[target] = scaled


def flip_kernel(held, out):
    for slot in range(held.shape[0]):
        out[slot] = held[slot].T


def second_kernel(places, counts, column, flipped, out):
    for tile in range(out.shape[0]):
        out[tile] = jnp.zeros(out.shape[1:], jnp.float32)
    for slot in range(flipped.shape[0]):
        left = column[place(places, 1, slot)]
        left = jnp.where(slot < counts[0, 0], left, jnp.zeros_like(left))
        target = place(places, 0, slot)
        out[target] += lax.dot_general(
            left, flipped[slot], (((1,), (0,)), ((), ())), preferred_element_type=jnp.float32
        )


def output_kernel(signal, both, first, second, low):
    cores, chips, _, _, width = both.shape
    for tile in range(chips * cores):
        span = slice(tile * width, (tile + 1) * width)
        walked = both[tile % cores, tile // cores, 0]
        lowpass = both[tile % cores, tile // cores, 1]
        first[:, span] = jnp.abs(signal[:, span] - walked)
        second[:, span] = jnp.abs(walked - lowpass)
        low[:, span] = lowpass


def in_vmem():
    return pl.BlockSpec(memory_space=pltpu.VMEM)


def in_smem():
    return pl.BlockSpec(memory_space=pltpu.SMEM)


def on_device(signal, tile_values, tile_places, tile_counts):
    channels, row_len = signal.shape
    slot_count, width = tile_values.shape[2:4]
    rows = row_len // width
    row_size = lax.axis_size(ROW)
    planes = row_size // LINES
    col_size = lax.axis_size(COL)
    halves = row_size // col_size
    params = pltpu.CompilerParams(vmem_limit_bytes=VMEM_BYTES)
    to_row = []
    for row in range(row_size):
        for col in range(col_size):
            piece = keeper((row % halves) * rows + col, rows, planes)
            source = (piece % planes) * LINES + piece // planes
            to_row.append((source * col_size + row // halves, row * col_size + col))

    held, degree_part, places = pl.pallas_call(
        functools.partial(degree_kernel, planes),
        out_shape=(
            pltpu.VMEM((slot_count, width, width), jnp.bfloat16),
            jax.ShapeDtypeStruct((col_size, rows, width), jnp.float32),
            pltpu.SMEM(tile_places.shape, jnp.int32),
        ),
        in_specs=[in_smem()] + [pl.BlockSpec(memory_space=pltpu.HBM)] * 2,
        out_specs=(in_vmem(), in_vmem(), in_smem()),
        scratch_shapes=[
            pltpu.VMEM((rows + 1, 8, width), jnp.float32),
            pltpu.SemaphoreType.DMA,
            pltpu.SemaphoreType.DMA((CHUNKS,)),
        ],
        compiler_params=params,
        name="degree",
    )(
        tile_counts,
        pltpu.with_memory_space_constraint(tile_places, pltpu.HBM),
        pltpu.with_memory_space_constraint(tile_values, pltpu.HBM),
    )
    gathered = exchange(degree_part, COL)

    partials = pl.pallas_call(
        functools.partial(first_kernel, halves),
        out_shape=jax.ShapeDtypeStruct((halves * rows * (channels + 1), width), jnp.float32),
        in_specs=[in_smem(), in_smem(), in_vmem(), in_vmem(), in_vmem()],
        out_specs=in_vmem(),
        scratch_shapes=[
            pltpu.VMEM((rows, channels, width), jnp.bfloat16),
            pltpu.VMEM((rows, width), jnp.float32),
            pltpu.VMEM((halves * rows, channels, width), jnp.float32),
        ],
        compiler_params=params,
        name="first",
    )(places, tile_counts, signal, gathered, held)
    received = exchange(partials.reshape(row_size, channels + 1, 1, width), ROW)
    walked_piece, scaled = pl.pallas_call(
        middle_kernel,
        out_shape=(
            jax.ShapeDtypeStruct((channels, width), jnp.float32),
            jax.ShapeDtypeStruct((row_size, channels, width), jnp.bfloat16),
        ),
        in_specs=[in_vmem()],
        out_specs=(in_vmem(), in_vmem()),
        compiler_params=params,
        name="middle",
    )(received.reshape(row_size * (channels + 1), width))

    scaled, held = lax.optimization_barrier((scaled, held))
    flipped = pl.pallas_call(
        flip_kernel,
        out_shape=pltpu.VMEM(held.shape, held.dtype),
        in_specs=[in_vmem()],
        out_specs=in_vmem(),
        input_output_aliases={0: 0},
        compiler_params=params,
        name="flip",
    )(held)
    column = exchange(scaled, ROW)
    walked_piece = lax.ppermute(walked_piece, ("plane", "line") + COL, to_row)
    partials = pl.pallas_call(
        second_kernel,
        out_shape=jax.ShapeDtypeStruct((rows, channels, width), jnp.float32),
        in_specs=[in_smem(), in_smem(), in_vmem(), in_vmem()],
        out_specs=in_vmem(),
        compiler_params=params,
        name="second",
    )(places, tile_counts, column, flipped)
    partials, walked_piece = lax.optimization_barrier((partials, walked_piece))
    spread = jnp.sum(exchange(partials, COL), axis=0)
    lowpass_piece = 0.5 * (walked_piece + spread)

    both = all_gather(jnp.stack([walked_piece, lowpass_piece]), "chip")
    both = lax.all_gather(both, "core")
    return pl.pallas_call(
        output_kernel,
        out_shape=(jax.ShapeDtypeStruct((channels, row_len), jnp.float32),) * 3,
        in_specs=[in_vmem(), in_vmem()],
        out_specs=(in_vmem(),) * 3,
        compiler_params=params,
        name="outputs",
    )(signal, both)


def solution(mesh):
    row_size, col_size = mesh.devices.shape
    shape = (row_size // LINES, LINES, col_size // CORES, CORES)
    mesh = Mesh(mesh.devices.reshape(shape), ("plane", "line") + COL)
    rows = ("plane", "line")
    in_specs = (
        P(None, rows),
        P(rows, COL, None, None, None),
        P(rows, COL, None, None),
        P(rows, COL),
    )
    out_specs = (P(None, rows), P(None, rows), P(None, rows))
    return jax.shard_map(
        on_device, mesh=mesh, in_specs=in_specs, out_specs=out_specs, check_vma=False
    )
```

```python
import functools

import jax
import jax.numpy as jnp
from jax import lax
from jax.experimental import pallas as pl
from jax.experimental.pallas import tpu as pltpu
from jax.sharding import Mesh, PartitionSpec as P

CHUNKS = 2
COPIES = 2
CORES = 2
LINES = 4
COL = ("chip", "core")
ROW = ("line", "plane")
VMEM_BYTES = 12 * 1024 * 1024


def exchange(partials, axis):
    return lax.all_to_all(partials, axis, 0, 0, tiled=True)


def all_gather(piece, axis):
    return exchange(jnp.broadcast_to(piece[None], (lax.axis_size(axis),) + piece.shape), axis)


def place(places, which, slot):
    return places[0, 0, which, slot]


def degree_kernel(counts, places_hbm, tiles, held, out, places, sums, small, sems):
    slot_count = tiles.shape[2]
    copy_places = pltpu.make_async_copy(places_hbm, places, small)
    copy_places.start()
    step = slot_count // CHUNKS
    copies = []
    part = step // COPIES
    for index in range(CHUNKS * COPIES):
        span = pl.ds(index * part, part)
        copies.append(pltpu.make_async_copy(tiles.at[0, 0, span], held.at[span], sems.at[index]))
        copies[-1].start()
    targets, rows, width = out.shape
    sums[...] = jnp.zeros_like(sums)
    ones = jnp.ones((8, width), jnp.bfloat16)
    copy_places.wait()
    for chunk in range(CHUNKS):
        for copy in copies[chunk * COPIES : (chunk + 1) * COPIES]:
            copy.wait()
        block = held[chunk * step : (chunk + 1) * step].reshape(step * width, width)
        found = lax.dot_general(
            ones, block, (((1,), (1,)), ((), ())), preferred_element_type=jnp.float32
        )
        for index in range(step):
            slot = chunk * step + index
            row = jnp.where(slot < counts[0, 0], place(places, 0, slot), rows)
            sums[row] += found[:, index * width : (index + 1) * width]
    for row in range(rows):
        for target in range(targets):
            out[target, row : row + 1, :] = sums[row, 0:1, :]


def first_kernel(halves, places, counts, signal, gathered, held, out, scaled, degree, sums):
    slot_count, width, _ = held.shape
    rows = gathered.shape[1]
    channels = signal.shape[0]
    row_index = lax.axis_index("plane") * LINES + lax.axis_index("line")
    col_index = lax.axis_index("chip") * CORES + lax.axis_index("core")
    total = gathered[0]
    for source in range(1, gathered.shape[0]):
        total += gathered[source]
    degree[...] = total
    for tile in range(rows):
        block = signal[:, tile * width : (tile + 1) * width]
        nodes = degree[tile : tile + 1, :]
        scaled[tile] = (block / nodes).astype(jnp.bfloat16)
        for half in range(halves):
            own = row_index == col_index * halves + half
            sums[half * rows + tile] = jnp.where(own, block, 0.0)
            end = (half * rows + tile + 1) * (channels + 1)
            out[end - 1 : end, :] = jnp.where(own, nodes, 0.0)
    for slot in range(slot_count):
        left = scaled[place(places, 0, slot)]
        left = jnp.where(slot < counts[0, 0], left, jnp.zeros_like(left))
        target = place(places, 1, slot)
        sums[target] += lax.dot_general(
            left, held[slot], (((1,), (0,)), ((), ())), preferred_element_type=jnp.float32
        )
    for tile in range(halves * rows):
        start = tile * (channels + 1)
        out[start : start + channels, :] = sums[tile]


def middle_kernel(received, walked, copies):
    channels = walked.shape[0]
    sources = received.shape[0] // (channels + 1)
    total, degree = 0.0, 0.0
    for source in range(sources):
        start = source * (channels + 1)
        total += received[start : start + channels, :]
        degree += received[start + channels : start + channels + 1, :]
    total = 0.5 * total
    walked[...] = total
    scaled = (total / degree).astype(jnp.bfloat16)
    for target in range(copies.shape[0]):
        copies[target] = scaled


def flip_kernel(held, out):
    for slot in range(held.shape[0]):
        out[slot] = held[slot].T


def second_kernel(places, counts, column, flipped, out):
    for tile in range(out.shape[0]):
        out[tile] = jnp.zeros(out.shape[1:], jnp.float32)
    for slot in range(flipped.shape[0]):
        left = column[place(places, 1, slot)]
        left = jnp.where(slot < counts[0, 0], left, jnp.zeros_like(left))
        target = place(places, 0, slot)
        out[target] += lax.dot_general(
            left, flipped[slot], (((1,), (0,)), ((), ())), preferred_element_type=jnp.float32
        )


def output_kernel(signal, both, first, second, low):
    cores, chips, _, _, width = both.shape
    for tile in range(chips * cores):
        span = slice(tile * width, (tile + 1) * width)
        walked = both[tile % cores, tile // cores, 0]
        lowpass = both[tile % cores, tile // cores, 1]
        first[:, span] = jnp.abs(signal[:, span] - walked)
        second[:, span] = jnp.abs(walked - lowpass)
        low[:, span] = lowpass


def in_vmem():
    return pl.BlockSpec(memory_space=pltpu.VMEM)


def in_smem():
    return pl.BlockSpec(memory_space=pltpu.SMEM)


def on_device(signal, tile_values, tile_places, tile_counts):
    channels, row_len = signal.shape
    slot_count, width = tile_values.shape[2:4]
    rows = row_len // width
    row_size = lax.axis_size(ROW)
    planes = row_size // LINES
    col_size = lax.axis_size(COL)
    halves = row_size // col_size
    params = pltpu.CompilerParams(vmem_limit_bytes=VMEM_BYTES)
    to_row = []
    for row in range(row_size):
        for col in range(col_size):
            piece = (row % halves) * rows + col
            source = (piece % planes) * LINES + piece // planes
            to_row.append((source * col_size + row // halves, row * col_size + col))

    held, degree_part, places = pl.pallas_call(
        degree_kernel,
        out_shape=(
            pltpu.VMEM((slot_count, width, width), jnp.bfloat16),
            jax.ShapeDtypeStruct((col_size, rows, width), jnp.float32),
            pltpu.SMEM(tile_places.shape, jnp.int32),
        ),
        in_specs=[in_smem()] + [pl.BlockSpec(memory_space=pltpu.HBM)] * 2,
        out_specs=(in_vmem(), in_vmem(), in_smem()),
        scratch_shapes=[
            pltpu.VMEM((rows + 1, 8, width), jnp.float32),
            pltpu.SemaphoreType.DMA,
            pltpu.SemaphoreType.DMA((CHUNKS * COPIES,)),
        ],
        compiler_params=params,
        name="degree",
    )(
        tile_counts,
        pltpu.with_memory_space_constraint(tile_places, pltpu.HBM),
        pltpu.with_memory_space_constraint(tile_values, pltpu.HBM),
    )
    gathered = exchange(degree_part, COL)

    partials = pl.pallas_call(
        functools.partial(first_kernel, halves),
        out_shape=jax.ShapeDtypeStruct((halves * rows * (channels + 1), width), jnp.float32),
        in_specs=[in_smem(), in_smem(), in_vmem(), in_vmem(), in_vmem()],
        out_specs=in_vmem(),
        scratch_shapes=[
            pltpu.VMEM((rows, channels, width), jnp.bfloat16),
            pltpu.VMEM((rows, width), jnp.float32),
            pltpu.VMEM((halves * rows, channels, width), jnp.float32),
        ],
        compiler_params=params,
        name="first",
    )(places, tile_counts, signal, gathered, held)
    received = exchange(partials.reshape(row_size, channels + 1, 1, width), ROW)
    walked_piece, scaled = pl.pallas_call(
        middle_kernel,
        out_shape=(
            jax.ShapeDtypeStruct((channels, width), jnp.float32),
            jax.ShapeDtypeStruct((row_size, channels, width), jnp.bfloat16),
        ),
        in_specs=[in_vmem()],
        out_specs=(in_vmem(), in_vmem()),
        compiler_params=params,
        name="middle",
    )(received.reshape(row_size * (channels + 1), width))

    scaled, held = lax.optimization_barrier((scaled, held))
    flipped = pl.pallas_call(
        flip_kernel,
        out_shape=pltpu.VMEM(held.shape, held.dtype),
        in_specs=[in_vmem()],
        out_specs=in_vmem(),
        input_output_aliases={0: 0},
        compiler_params=params,
        name="flip",
    )(held)
    column = exchange(scaled, ROW)
    walked_piece = lax.ppermute(walked_piece, ("plane", "line") + COL, to_row)
    partials = pl.pallas_call(
        second_kernel,
        out_shape=jax.ShapeDtypeStruct((rows, channels, width), jnp.float32),
        in_specs=[in_smem(), in_smem(), in_vmem(), in_vmem()],
        out_specs=in_vmem(),
        compiler_params=params,
        name="second",
    )(places, tile_counts, column, flipped)
    partials, walked_piece = lax.optimization_barrier((partials, walked_piece))
    spread = jnp.sum(exchange(partials, COL), axis=0)
    lowpass_piece = 0.5 * (walked_piece + spread)

    both = all_gather(jnp.stack([walked_piece, lowpass_piece]), "chip")
    both = lax.all_gather(both, "core")
    return pl.pallas_call(
        output_kernel,
        out_shape=(jax.ShapeDtypeStruct((channels, row_len), jnp.float32),) * 3,
        in_specs=[in_vmem(), in_vmem()],
        out_specs=(in_vmem(),) * 3,
        compiler_params=params,
        name="outputs",
    )(signal, both)


def solution(mesh):
    row_size, col_size = mesh.devices.shape
    shape = (row_size // LINES, LINES, col_size // CORES, CORES)
    mesh = Mesh(mesh.devices.reshape(shape), ("plane", "line") + COL)
    rows = ("plane", "line")
    in_specs = (
        P(None, rows),
        P(rows, COL, None, None, None),
        P(rows, COL, None, None),
        P(rows, COL),
    )
    out_specs = (P(None, rows), P(None, rows), P(None, rows))
    return jax.shard_map(
        on_device, mesh=mesh, in_specs=in_specs, out_specs=out_specs, check_vma=False
    )
```
